128 devices in a mesh: row: 16 (over x, z_hi, core), col: 8 (over y, z_lo).
Axes of the slice: x: 4, y: 4, z: 4 (z_hi: 2, z_lo: 2; z = z_hi * 2 + z_lo), core: 2. Of those that a mesh axis runs over, the one named last changes fastest.
Arguments:
- features: bfloat16 [1024, 128], P(('row', 'col')), may hold values from -6 to 6
- row_weight: bfloat16 [128, 32], replicated, may hold values from -0.5 to 0.5
- col_weight: bfloat16 [128, 32], replicated, may hold values from -0.5 to 0.5
- conv_weight: bfloat16 [2, 9, 64, 64], replicated, may hold values from -0.25 to 0.25
- conv_bias: float32 [2, 64], replicated, may hold values from -3 to 3
- dilations: int32 [2], replicated, may hold values from 1 to 4, as said below
Outputs:
- pair_map: bfloat16 [64, 1024, 1024], P(None, 'row', 'col')
The draws below stay inside these ranges and needn't reach their ends.
Inputs may be any that keep to these rules, and one draw needn't show every extreme that they name: `dilations`: one dilation a layer; at least one layer uses exactly 4.
All inputs are finite; a program needn't handle non-finite values.
Results may differ from the reference program's by a relative error of at most 0.008.
Values may be sent and summed in bfloat16 or wider, within the bound.
A program may use at most 64 MiB of HBM per device.

```python
import jax
import jax.numpy as jnp
from jax import lax

CH = 64
FEAT = 128
HALF = 32
BINS = 1024
LAYERS = 2
MAXDIL = 4


def draw_dilations(key, part):
    key_rates, key_pick = jax.random.split(key)
    drawn_rates = jax.random.randint(key_rates, (LAYERS,), 1, MAXDIL + 1)
    chosen = jax.random.randint(key_pick, (), 0, LAYERS)
    return jnp.where(jnp.arange(LAYERS) == chosen, MAXDIL, drawn_rates).astype(jnp.int32)


def levels(stream_key, shape, pieces, smallest, top_value):
    def one(position, blocks):
        heights = jax.random.uniform(jax.random.fold_in(jax.random.fold_in(stream_key, 6), position), (blocks,), jnp.float32, smallest / len(pieces), top_value / len(pieces))
        return jnp.repeat(jnp.exp(heights), shape[position] // blocks).reshape((-1,) + (1,) * (len(shape) - position - 1))

    level = one(*pieces[0])
    for cut in pieces[1:]:
        level = level * one(*cut)
    return level


def noise(key, dims, deviation, bound, cuts=(), kind=jnp.bfloat16):
    entries = jax.random.normal(key, dims, jnp.float32) * deviation
    if len(cuts) > 0:
        entries = levels(key, dims, cuts, -0.22, 0.18) * entries
    return jnp.clip(entries, min=-bound, max=bound).astype(kind)


def setup_inputs(seed: int = 0) -> dict:
    splits = jax.random.split(jax.random.key(seed), 7)
    return {
        "features": noise(splits[0], (BINS, FEAT), 1.0, 6.0, ((0, 128),)),
        "row_weight": noise(splits[1], (FEAT, HALF), FEAT ** -0.5, 0.5),
        "col_weight": noise(splits[2], (FEAT, HALF), FEAT ** -0.5, 0.5),
        "conv_weight": noise(splits[3], (LAYERS, 9, CH, CH), (9 * CH) ** -0.5, 0.25),
        "conv_bias": noise(splits[4], (LAYERS, CH), 0.5, 3.0, (), jnp.float32),
        "dilations": draw_dilations(jax.random.fold_in(splits[6], 71), 0),
    }


def dilated_layer(pair_now, weights, shift_bias, dilation):
    channels = pair_now.shape[0]
    length = pair_now.shape[1]
    block_rows = 128
    active = jax.nn.relu(pair_now)
    padded = jnp.pad(active, ((0, 0), (MAXDIL, MAXDIL), (MAXDIL, MAXDIL)))
    weights_wide = weights.astype(jnp.float32)
    zero_index = jnp.zeros((), jnp.int32)
    dilation = dilation.astype(jnp.int32)

    def one_block(block_index):
        first_row = (block_index * block_rows).astype(jnp.int32)
        summed = jnp.zeros((channels, block_rows, length), jnp.float32)
        for kernel_tap in range(9):
            row_step = kernel_tap // 3 - 1
            col_step = kernel_tap % 3 - 1
            row_index = (first_row + MAXDIL + row_step * dilation).astype(jnp.int32)
            col_index = (MAXDIL + col_step * dilation).astype(jnp.int32)
            shifted = lax.dynamic_slice(padded, (zero_index, row_index, col_index), (channels, block_rows, length))
            summed = summed + jnp.einsum("ok,kij->oij", weights_wide[kernel_tap], shifted.astype(jnp.float32))
        own_rows = lax.dynamic_slice_in_dim(pair_now, first_row, block_rows, 1).astype(jnp.float32)
        return (own_rows + shift_bias[:, None, None] + summed).astype(jnp.bfloat16)

    blocks = lax.map(one_block, jnp.arange(length // block_rows).astype(jnp.int32))
    return jnp.transpose(blocks, (1, 0, 2, 3)).reshape(channels, length, length)


def symmetrize(mixed_map):
    channels = mixed_map.shape[0]
    length = mixed_map.shape[1]
    block_rows = 128

    def one_block(block_index):
        first_row = (block_index * block_rows).astype(jnp.int32)
        own_rows = lax.dynamic_slice_in_dim(mixed_map, first_row, block_rows, 1).astype(jnp.float32)
        own_cols = lax.dynamic_slice_in_dim(mixed_map, first_row, block_rows, 2).astype(jnp.float32)
        return (0.5 * (own_rows + jnp.swapaxes(own_cols, 1, 2))).astype(jnp.bfloat16)

    blocks = lax.map(one_block, jnp.arange(length // block_rows).astype(jnp.int32))
    return jnp.transpose(blocks, (1, 0, 2, 3)).reshape(channels, length, length)


def reference(features, row_weight, col_weight, conv_weight, conv_bias, dilations):
    row_proj = jnp.dot(features, row_weight, preferred_element_type=jnp.float32).astype(jnp.bfloat16)
    col_proj = jnp.dot(features, col_weight, preferred_element_type=jnp.float32).astype(jnp.bfloat16)
    length = features.shape[0]
    half_width = row_proj.shape[1]
    upper = jnp.broadcast_to(row_proj.T[:, :, None], (half_width, length, length))
    lower = jnp.broadcast_to(col_proj.T[:, None, :], (half_width, length, length))
    pair_now = jnp.concatenate([upper, lower], axis=0)
    for layer_index in range(LAYERS):
        mixed_map = dilated_layer(pair_now, conv_weight[layer_index], conv_bias[layer_index], dilations[layer_index])
        mixed_map = lax.optimization_barrier(mixed_map)
        pair_now = symmetrize(mixed_map)
    return pair_now
```

```python
import jax
import jax.numpy as jnp
from jax import lax
from jax.sharding import PartitionSpec as P

MAXDIL = 4
REACH = 2 * MAXDIL


def gather_projections(proj):
    along_col = lax.all_gather(proj, "col", axis=0, tiled=True)
    return lax.all_gather(along_col, "row", axis=0, tiled=True)


def inside(start, count, bins_total):
    places = jnp.arange(count) + start
    return (places >= 0) & (places < bins_total)


def dilated_conv(act, kernel, dilation, out_rows, out_cols, margin):
    def branch(d):
        def run(x):
            lo = margin - d
            piece = x[:, lo : lo + out_rows + 2 * d, lo : lo + out_cols + 2 * d]
            return lax.conv_general_dilated(
                piece[None],
                kernel,
                window_strides=(1, 1),
                padding="VALID",
                rhs_dilation=(d, d),
                dimension_numbers=("NCHW", "OIHW", "NCHW"),
                preferred_element_type=jnp.float32,
            )[0]

        return run

    return lax.switch(dilation - 1, [branch(d) for d in range(1, MAXDIL + 1)], act)


def as_kernel(taps):
    out_ch, in_ch = taps.shape[1], taps.shape[2]
    return jnp.transpose(taps.reshape(3, 3, out_ch, in_ch), (2, 3, 0, 1))


def turned(kernel):
    return jnp.swapaxes(kernel, 2, 3)


def local(features, row_weight, col_weight, conv_weight, conv_bias, dilations):
    half = row_weight.shape[1]
    both = jnp.concatenate([row_weight, col_weight], axis=1)
    proj = jnp.dot(features, both, preferred_element_type=jnp.float32).astype(jnp.bfloat16)
    every = gather_projections(proj)
    bins_total = every.shape[0]
    row_size = bins_total // lax.axis_size("row")
    col_size = bins_total // lax.axis_size("col")
    row_start = lax.axis_index("row") * row_size
    col_start = lax.axis_index("col") * col_size

    padded = jnp.pad(every, ((REACH, REACH), (0, 0)))
    rows_ext = row_size + 2 * REACH
    cols_ext = col_size + 2 * REACH
    at_rows = lax.dynamic_slice_in_dim(padded, row_start, rows_ext, 0)
    at_cols = lax.dynamic_slice_in_dim(padded, col_start, cols_ext, 0)
    shape0 = (half, rows_ext, cols_ext)
    map0 = jnp.concatenate(
        [
            jnp.broadcast_to(at_rows[:, :half].T[:, :, None], shape0),
            jnp.broadcast_to(at_cols[:, half:].T[:, None, :], shape0),
        ],
        axis=0,
    )
    map0_mirror = jnp.concatenate(
        [
            jnp.broadcast_to(at_cols[:, :half].T[:, None, :], shape0),
            jnp.broadcast_to(at_rows[:, half:].T[:, :, None], shape0),
        ],
        axis=0,
    )
    row_in = inside(row_start - REACH, rows_ext, bins_total)
    col_in = inside(col_start - REACH, cols_ext, bins_total)
    mask0 = (row_in[:, None] & col_in[None, :]).astype(jnp.bfloat16)

    kernel0 = as_kernel(conv_weight[0])
    rows1 = row_size + 2 * MAXDIL
    cols1 = col_size + 2 * MAXDIL
    conv0 = dilated_conv(jax.nn.relu(map0) * mask0, kernel0, dilations[0], rows1, cols1, MAXDIL)
    conv0_mirror = dilated_conv(
        jax.nn.relu(map0_mirror) * mask0, turned(kernel0), dilations[0], rows1, cols1, MAXDIL
    )
    bias0 = conv_bias[0][:, None, None]
    core0 = (slice(None), slice(MAXDIL, MAXDIL + rows1), slice(MAXDIL, MAXDIL + cols1))
    mixed0 = (map0[core0].astype(jnp.float32) + bias0 + conv0).astype(jnp.bfloat16)
    mixed0_mirror = (map0_mirror[core0].astype(jnp.float32) + bias0 + conv0_mirror).astype(
        jnp.bfloat16
    )
    map1 = (0.5 * (mixed0.astype(jnp.float32) + mixed0_mirror.astype(jnp.float32))).astype(
        jnp.bfloat16
    )

    mask1 = mask0[MAXDIL : MAXDIL + rows1, MAXDIL : MAXDIL + cols1]
    kernel1 = as_kernel(conv_weight[1])
    kernel1_both = jnp.concatenate([kernel1, turned(kernel1)], axis=0)
    conv1 = dilated_conv(
        jax.nn.relu(map1) * mask1, kernel1_both, dilations[1], row_size, col_size, MAXDIL
    )
    channels = kernel1.shape[0]
    core1 = (slice(None), slice(MAXDIL, MAXDIL + row_size), slice(MAXDIL, MAXDIL + col_size))
    base1 = map1[core1].astype(jnp.float32) + conv_bias[1][:, None, None]
    mixed1 = (base1 + conv1[:channels]).astype(jnp.bfloat16)
    mixed1_mirror = (base1 + conv1[channels:]).astype(jnp.bfloat16)
    return (0.5 * (mixed1.astype(jnp.float32) + mixed1_mirror.astype(jnp.float32))).astype(
        jnp.bfloat16
    )


def solution(mesh):
    placed = (P(("row", "col"), None), P(), P(), P(), P(), P())
    return jax.shard_map(
        local, mesh=mesh, in_specs=placed, out_specs=P(None, "row", "col"), check_vma=False
    )
```

```python
import jax
import jax.numpy as jnp
from jax import lax
from jax.sharding import PartitionSpec as P

MAXDIL = 4
REACH = 2 * MAXDIL


def gather_projections(proj):
    along_col = lax.all_gather(proj, "col", axis=0, tiled=True)
    return lax.all_gather(along_col, "row", axis=0, tiled=True)


def inside(places, bins_total):
    return ((places >= 0) & (places < bins_total)).astype(jnp.float32)


def tap_groups(padded, weights, dilation):
    out_channels = weights.shape[1]
    in_channels = weights.shape[2]
    row_count = padded.shape[1] - 2 * MAXDIL
    col_count = padded.shape[2] - 2 * MAXDIL
    zero_index = jnp.zeros((), jnp.int32)
    summed = jnp.zeros((out_channels, row_count * col_count), jnp.float32)
    for group_index in range(3):
        row_step = group_index - 1
        pieces = []
        for inner_index in range(3):
            col_step = inner_index - 1
            row_index = MAXDIL + row_step * dilation
            col_index = MAXDIL + col_step * dilation
            pieces.append(
                lax.dynamic_slice(
                    padded, (zero_index, row_index, col_index), (in_channels, row_count, col_count)
                )
            )
        stacked = jnp.concatenate(pieces, axis=0).reshape(3 * in_channels, row_count * col_count)
        group_weight = jnp.transpose(
            weights[3 * group_index : 3 * group_index + 3], (1, 0, 2)
        ).reshape(out_channels, 3 * in_channels)
        summed = summed + jnp.dot(group_weight, stacked, preferred_element_type=jnp.float32)
    return summed.reshape(out_channels, row_count, col_count)


def mirrored_taps(weights):
    return weights.reshape(3, 3, *weights.shape[1:]).swapaxes(0, 1).reshape(weights.shape)


def first_layer(every, taps, shift_bias, dilation, row_start, rows, col_start, cols):
    bins_total = every.shape[0]
    half = every.shape[1] // 2
    active = jnp.pad(jax.nn.relu(every), ((REACH, REACH), (0, 0)))
    row_part = jnp.einsum(
        "nk,tok->tno", active[:, :half], taps[:, :, :half], preferred_element_type=jnp.float32
    )
    col_part = jnp.einsum(
        "nk,tok->tno", active[:, half:], taps[:, :, half:], preferred_element_type=jnp.float32
    )
    span = bins_total + 2 * MAXDIL
    by_col, by_row = [], []
    for outer in range(3):
        along_rows = None
        along_cols = None
        for inner in range(3):
            piece_r = lax.dynamic_slice_in_dim(
                row_part[3 * inner + outer], MAXDIL + (inner - 1) * dilation, span, 0
            )
            piece_c = lax.dynamic_slice_in_dim(
                col_part[3 * outer + inner], MAXDIL + (inner - 1) * dilation, span, 0
            )
            along_rows = piece_r if along_rows is None else along_rows + piece_r
            along_cols = piece_c if along_cols is None else along_cols + piece_c
        by_col.append(along_rows)
        by_row.append(along_cols)

    def at(table, start, count):
        return lax.dynamic_slice_in_dim(table, start, count, 0)

    row_places = row_start - MAXDIL + jnp.arange(rows)
    col_places = col_start - MAXDIL + jnp.arange(cols)

    def conv_at(p_start, p_places, q_start, q_places, p_count, q_count, p_axis):
        total = None
        for step in range(3):
            q_in = inside(q_places + (step - 1) * dilation, bins_total)
            p_in = inside(p_places + (step - 1) * dilation, bins_total)
            term_p = at(by_col[step], p_start, p_count).T
            term_q = at(by_row[step], q_start, q_count).T
            if p_axis == 1:
                piece = term_p[:, :, None] * q_in[None, None, :] + term_q[:, None, :] * p_in[
                    None, :, None
                ]
            else:
                piece = term_p[:, None, :] * q_in[None, :, None] + term_q[:, :, None] * p_in[
                    None, None, :
                ]
            total = piece if total is None else total + piece
        return total

    padded = jnp.pad(every, ((MAXDIL, MAXDIL), (0, 0)))
    rows_here = at(padded, row_start, rows)
    cols_here = at(padded, col_start, cols)
    shape = (half, rows, cols)
    map0 = jnp.concatenate(
        [
            jnp.broadcast_to(rows_here[:, :half].T[:, :, None], shape),
            jnp.broadcast_to(cols_here[:, half:].T[:, None, :], shape),
        ],
        axis=0,
    )
    map0_mirror = jnp.concatenate(
        [
            jnp.broadcast_to(cols_here[:, :half].T[:, None, :], shape),
            jnp.broadcast_to(rows_here[:, half:].T[:, :, None], shape),
        ],
        axis=0,
    )
    bias = shift_bias[:, None, None]
    conv = conv_at(row_start, row_places, col_start, col_places, rows, cols, 1)
    conv_mirror = conv_at(col_start, col_places, row_start, row_places, cols, rows, 2)
    mixed = (map0.astype(jnp.float32) + bias + conv).astype(jnp.bfloat16)
    mixed_mirror = (map0_mirror.astype(jnp.float32) + bias + conv_mirror).astype(jnp.bfloat16)
    return mixed, mixed_mirror, row_places, col_places


def local(features, row_weight, col_weight, conv_weight, conv_bias, dilations):
    both = jnp.concatenate([row_weight, col_weight], axis=1)
    proj = jnp.dot(features, both, preferred_element_type=jnp.float32).astype(jnp.bfloat16)
    every = gather_projections(proj)
    bins_total = every.shape[0]
    row_size = bins_total // lax.axis_size("row")
    col_size = bins_total // lax.axis_size("col")
    row_start = lax.axis_index("row") * row_size
    col_start = lax.axis_index("col") * col_size
    rows1 = row_size + 2 * MAXDIL
    cols1 = col_size + 2 * MAXDIL

    mixed0, mixed0_mirror, row_places, col_places = first_layer(
        every, conv_weight[0], conv_bias[0], dilations[0], row_start, rows1, col_start, cols1
    )
    map1 = (0.5 * (mixed0.astype(jnp.float32) + mixed0_mirror.astype(jnp.float32))).astype(
        jnp.bfloat16
    )

    mask1 = (
        inside(row_places, bins_total)[:, None] * inside(col_places, bins_total)[None, :]
    ).astype(jnp.bfloat16)
    taps1 = jnp.concatenate([conv_weight[1], mirrored_taps(conv_weight[1])], axis=1)
    conv1 = tap_groups(jax.nn.relu(map1) * mask1, taps1, dilations[1])
    channels = conv_weight.shape[2]
    core = (slice(None), slice(MAXDIL, MAXDIL + row_size), slice(MAXDIL, MAXDIL + col_size))
    base1 = map1[core].astype(jnp.float32) + conv_bias[1][:, None, None]
    mixed1 = (base1 + conv1[:channels]).astype(jnp.bfloat16)
    mixed1_mirror = (base1 + conv1[channels:]).astype(jnp.bfloat16)
    return (0.5 * (mixed1.astype(jnp.float32) + mixed1_mirror.astype(jnp.float32))).astype(
        jnp.bfloat16
    )


def solution(mesh):
    placed = (P(("row", "col"), None), P(), P(), P(), P(), P())
    return jax.shard_map(
        local, mesh=mesh, in_specs=placed, out_specs=P(None, "row", "col"), check_vma=False
    )
```

```python
import jax
import jax.numpy as jnp
from jax import lax
from jax.sharding import PartitionSpec as P

MAXDIL = 4
REACH = 2 * MAXDIL


def gather_projections(proj):
    axes = ("row", "col")
    count = lax.axis_size("row") * lax.axis_size("col")
    copies = jnp.broadcast_to(proj[None], (count,) + proj.shape)
    return lax.all_to_all(copies, axes, 0, 0, tiled=True).reshape(-1, proj.shape[1])


def inside(places, bins_total):
    return ((places >= 0) & (places < bins_total)).astype(jnp.float32)


def tap_groups(padded, weights, dilation):
    out_channels = weights.shape[1]
    in_channels = weights.shape[2]
    row_count = padded.shape[1] - 2 * MAXDIL
    col_count = padded.shape[2] - 2 * MAXDIL
    zero_index = jnp.zeros((), jnp.int32)
    summed = jnp.zeros((out_channels, row_count * col_count), jnp.float32)
    for group_index in range(3):
        row_step = group_index - 1
        pieces = []
        for inner_index in range(3):
            col_step = inner_index - 1
            row_index = MAXDIL + row_step * dilation
            col_index = MAXDIL + col_step * dilation
            pieces.append(
                lax.dynamic_slice(
                    padded, (zero_index, row_index, col_index), (in_channels, row_count, col_count)
                )
            )
        stacked = jnp.concatenate(pieces, axis=0).reshape(3 * in_channels, row_count * col_count)
        group_weight = jnp.transpose(
            weights[3 * group_index : 3 * group_index + 3], (1, 0, 2)
        ).reshape(out_channels, 3 * in_channels)
        summed = summed + jnp.dot(group_weight, stacked, preferred_element_type=jnp.float32)
    return summed.reshape(out_channels, row_count, col_count)


def mirrored_taps(weights):
    return weights.reshape(3, 3, *weights.shape[1:]).swapaxes(0, 1).reshape(weights.shape)


def first_layer(every, taps, shift_bias, dilation, row_start, rows, col_start, cols):
    bins_total = every.shape[0]
    half = every.shape[1] // 2
    active = jnp.pad(jax.nn.relu(every), ((REACH, REACH), (0, 0)))
    row_part = jnp.einsum(
        "nk,tok->tno", active[:, :half], taps[:, :, :half], preferred_element_type=jnp.float32
    )
    col_part = jnp.einsum(
        "nk,tok->tno", active[:, half:], taps[:, :, half:], preferred_element_type=jnp.float32
    )
    span = bins_total + 2 * MAXDIL
    by_col, by_row = [], []
    for outer in range(3):
        along_rows = None
        along_cols = None
        for inner in range(3):
            piece_r = lax.dynamic_slice_in_dim(
                row_part[3 * inner + outer], MAXDIL + (inner - 1) * dilation, span, 0
            )
            piece_c = lax.dynamic_slice_in_dim(
                col_part[3 * outer + inner], MAXDIL + (inner - 1) * dilation, span, 0
            )
            along_rows = piece_r if along_rows is None else along_rows + piece_r
            along_cols = piece_c if along_cols is None else along_cols + piece_c
        by_col.append(along_rows)
        by_row.append(along_cols)

    def at(table, start, count):
        return lax.dynamic_slice_in_dim(table, start, count, 0)

    row_places = row_start - MAXDIL + jnp.arange(rows)
    col_places = col_start - MAXDIL + jnp.arange(cols)

    def conv_at(p_start, p_places, q_start, q_places, p_count, q_count, p_axis):
        total = None
        for step in range(3):
            q_in = inside(q_places + (step - 1) * dilation, bins_total)
            p_in = inside(p_places + (step - 1) * dilation, bins_total)
            term_p = at(by_col[step], p_start, p_count).T
            term_q = at(by_row[step], q_start, q_count).T
            if p_axis == 1:
                piece = term_p[:, :, None] * q_in[None, None, :] + term_q[:, None, :] * p_in[
                    None, :, None
                ]
            else:
                piece = term_p[:, None, :] * q_in[None, :, None] + term_q[:, :, None] * p_in[
                    None, None, :
                ]
            total = piece if total is None else total + piece
        return total

    padded = jnp.pad(every, ((MAXDIL, MAXDIL), (0, 0)))
    rows_here = at(padded, row_start, rows)
    cols_here = at(padded, col_start, cols)
    shape = (half, rows, cols)
    map0 = jnp.concatenate(
        [
            jnp.broadcast_to(rows_here[:, :half].T[:, :, None], shape),
            jnp.broadcast_to(cols_here[:, half:].T[:, None, :], shape),
        ],
        axis=0,
    )
    map0_mirror = jnp.concatenate(
        [
            jnp.broadcast_to(cols_here[:, :half].T[:, None, :], shape),
            jnp.broadcast_to(rows_here[:, half:].T[:, :, None], shape),
        ],
        axis=0,
    )
    bias = shift_bias[:, None, None]
    conv = conv_at(row_start, row_places, col_start, col_places, rows, cols, 1)
    conv_mirror = conv_at(col_start, col_places, row_start, row_places, cols, rows, 2)
    mixed = (map0.astype(jnp.float32) + bias + conv).astype(jnp.bfloat16)
    mixed_mirror = (map0_mirror.astype(jnp.float32) + bias + conv_mirror).astype(jnp.bfloat16)
    return mixed, mixed_mirror, row_places, col_places


def local(features, row_weight, col_weight, conv_weight, conv_bias, dilations):
    both = jnp.concatenate([row_weight, col_weight], axis=1)
    proj = jnp.dot(features, both, preferred_element_type=jnp.float32).astype(jnp.bfloat16)
    every = gather_projections(proj)
    bins_total = every.shape[0]
    row_size = bins_total // lax.axis_size("row")
    col_size = bins_total // lax.axis_size("col")
    row_start = lax.axis_index("row") * row_size
    col_start = lax.axis_index("col") * col_size
    rows1 = row_size + 2 * MAXDIL
    cols1 = col_size + 2 * MAXDIL

    mixed0, mixed0_mirror, row_places, col_places = first_layer(
        every, conv_weight[0], conv_bias[0], dilations[0], row_start, rows1, col_start, cols1
    )
    map1 = (0.5 * (mixed0.astype(jnp.float32) + mixed0_mirror.astype(jnp.float32))).astype(
        jnp.bfloat16
    )

    mask1 = (
        inside(row_places, bins_total)[:, None] * inside(col_places, bins_total)[None, :]
    ).astype(jnp.bfloat16)
    taps1 = jnp.concatenate([conv_weight[1], mirrored_taps(conv_weight[1])], axis=1)
    conv1 = tap_groups(jax.nn.relu(map1) * mask1, taps1, dilations[1])
    channels = conv_weight.shape[2]
    core = (slice(None), slice(MAXDIL, MAXDIL + row_size), slice(MAXDIL, MAXDIL + col_size))
    base1 = map1[core].astype(jnp.float32) + conv_bias[1][:, None, None]
    mixed1 = (base1 + conv1[:channels]).astype(jnp.bfloat16)
    mixed1_mirror = (base1 + conv1[channels:]).astype(jnp.bfloat16)
    return (0.5 * (mixed1.astype(jnp.float32) + mixed1_mirror.astype(jnp.float32))).astype(
        jnp.bfloat16
    )


def solution(mesh):
    placed = (P(("row", "col"), None), P(), P(), P(), P(), P())
    return jax.shard_map(
        local, mesh=mesh, in_specs=placed, out_specs=P(None, "row", "col"), check_vma=False
    )
```

```python
import jax
import jax.numpy as jnp
from jax import lax
from jax.sharding import PartitionSpec as P

MAXDIL = 4
REACH = 2 * MAXDIL


def gather_projections(proj):
    axes = ("row", "col")
    count = lax.axis_size("row") * lax.axis_size("col")
    copies = jnp.broadcast_to(proj[None], (count,) + proj.shape)
    return lax.all_to_all(copies, axes, 0, 0, tiled=True).reshape(-1, proj.shape[1])


def inside(places, bins_total):
    return ((places >= 0) & (places < bins_total)).astype(jnp.float32)


def tap_groups(padded, weights, dilation):
    out_channels = weights.shape[1]
    in_channels = weights.shape[2]
    row_count = padded.shape[1] - 2 * MAXDIL
    col_count = padded.shape[2] - 2 * MAXDIL
    summed = jnp.zeros((out_channels, row_count * col_count), jnp.float32)
    for group_index in range(3):
        row_step = group_index - 1
        pieces = []
        for inner_index in range(3):
            col_step = inner_index - 1
            row_index = MAXDIL + row_step * dilation
            col_index = MAXDIL + col_step * dilation
            pieces.append(
                padded[:, row_index : row_index + row_count, col_index : col_index + col_count]
            )
        stacked = jnp.concatenate(pieces, axis=0).reshape(3 * in_channels, row_count * col_count)
        group_weight = jnp.transpose(
            weights[3 * group_index : 3 * group_index + 3], (1, 0, 2)
        ).reshape(out_channels, 3 * in_channels)
        summed = summed + jnp.dot(group_weight, stacked, preferred_element_type=jnp.float32)
    return summed.reshape(out_channels, row_count, col_count)


def mirrored_taps(weights):
    return weights.reshape(3, 3, *weights.shape[1:]).swapaxes(0, 1).reshape(weights.shape)


def first_layer(every, taps, shift_bias, dilation, row_start, rows, col_start, cols):
    bins_total = every.shape[0]
    half = every.shape[1] // 2
    active = jnp.pad(jax.nn.relu(every), ((REACH, REACH), (0, 0)))
    row_part = jnp.einsum(
        "nk,tok->tno", active[:, :half], taps[:, :, :half], preferred_element_type=jnp.float32
    )
    col_part = jnp.einsum(
        "nk,tok->tno", active[:, half:], taps[:, :, half:], preferred_element_type=jnp.float32
    )
    span = bins_total + 2 * MAXDIL
    by_col, by_row = [], []
    for outer in range(3):
        along_rows = None
        along_cols = None
        for inner in range(3):
            piece_r = lax.dynamic_slice_in_dim(
                row_part[3 * inner + outer], MAXDIL + (inner - 1) * dilation, span, 0
            )
            piece_c = lax.dynamic_slice_in_dim(
                col_part[3 * outer + inner], MAXDIL + (inner - 1) * dilation, span, 0
            )
            along_rows = piece_r if along_rows is None else along_rows + piece_r
            along_cols = piece_c if along_cols is None else along_cols + piece_c
        by_col.append(along_rows)
        by_row.append(along_cols)

    def at(table, start, count):
        return lax.dynamic_slice_in_dim(table, start, count, 0)

    row_places = row_start - MAXDIL + jnp.arange(rows)
    col_places = col_start - MAXDIL + jnp.arange(cols)

    def conv_at(p_start, p_places, q_start, q_places, p_count, q_count, p_axis):
        total = None
        for step in range(3):
            q_in = inside(q_places + (step - 1) * dilation, bins_total)
            p_in = inside(p_places + (step - 1) * dilation, bins_total)
            term_p = at(by_col[step], p_start, p_count).T
            term_q = at(by_row[step], q_start, q_count).T
            if p_axis == 1:
                piece = term_p[:, :, None] * q_in[None, None, :] + term_q[:, None, :] * p_in[
                    None, :, None
                ]
            else:
                piece = term_p[:, None, :] * q_in[None, :, None] + term_q[:, :, None] * p_in[
                    None, None, :
                ]
            total = piece if total is None else total + piece
        return total

    padded = jnp.pad(every, ((MAXDIL, MAXDIL), (0, 0)))
    rows_here = at(padded, row_start, rows)
    cols_here = at(padded, col_start, cols)
    shape = (half, rows, cols)
    map0 = jnp.concatenate(
        [
            jnp.broadcast_to(rows_here[:, :half].T[:, :, None], shape),
            jnp.broadcast_to(cols_here[:, half:].T[:, None, :], shape),
        ],
        axis=0,
    )
    map0_mirror = jnp.concatenate(
        [
            jnp.broadcast_to(cols_here[:, :half].T[:, None, :], shape),
            jnp.broadcast_to(rows_here[:, half:].T[:, :, None], shape),
        ],
        axis=0,
    )
    bias = shift_bias[:, None, None]
    conv = conv_at(row_start, row_places, col_start, col_places, rows, cols, 1)
    conv_mirror = conv_at(col_start, col_places, row_start, row_places, cols, rows, 2)
    mixed = (map0.astype(jnp.float32) + bias + conv).astype(jnp.bfloat16)
    mixed_mirror = (map0_mirror.astype(jnp.float32) + bias + conv_mirror).astype(jnp.bfloat16)
    return mixed, mixed_mirror, row_places, col_places


def local(features, row_weight, col_weight, conv_weight, conv_bias, dilations):
    both = jnp.concatenate([row_weight, col_weight], axis=1)
    proj = jnp.dot(features, both, preferred_element_type=jnp.float32).astype(jnp.bfloat16)
    every = gather_projections(proj)
    bins_total = every.shape[0]
    row_size = bins_total // lax.axis_size("row")
    col_size = bins_total // lax.axis_size("col")
    row_start = lax.axis_index("row") * row_size
    col_start = lax.axis_index("col") * col_size
    rows1 = row_size + 2 * MAXDIL
    cols1 = col_size + 2 * MAXDIL

    mixed0, mixed0_mirror, row_places, col_places = first_layer(
        every, conv_weight[0], conv_bias[0], dilations[0], row_start, rows1, col_start, cols1
    )
    map1 = (0.5 * (mixed0.astype(jnp.float32) + mixed0_mirror.astype(jnp.float32))).astype(
        jnp.bfloat16
    )

    mask1 = (
        inside(row_places, bins_total)[:, None] * inside(col_places, bins_total)[None, :]
    ).astype(jnp.bfloat16)
    taps1 = jnp.concatenate([conv_weight[1], mirrored_taps(conv_weight[1])], axis=1)
    conv1 = lax.switch(
        dilations[1] - 1,
        [lambda act, w, d=d: tap_groups(act, w, d) for d in range(1, MAXDIL + 1)],
        jax.nn.relu(map1) * mask1,
        taps1,
    )
    channels = conv_weight.shape[2]
    core = (slice(None), slice(MAXDIL, MAXDIL + row_size), slice(MAXDIL, MAXDIL + col_size))
    base1 = map1[core].astype(jnp.float32) + conv_bias[1][:, None, None]
    mixed1 = (base1 + conv1[:channels]).astype(jnp.bfloat16)
    mixed1_mirror = (base1 + conv1[channels:]).astype(jnp.bfloat16)
    return (0.5 * (mixed1.astype(jnp.float32) + mixed1_mirror.astype(jnp.float32))).astype(
        jnp.bfloat16
    )


def solution(mesh):
    placed = (P(("row", "col"), None), P(), P(), P(), P(), P())
    return jax.shard_map(
        local, mesh=mesh, in_specs=placed, out_specs=P(None, "row", "col"), check_vma=False
    )
```

```python
import jax
import jax.numpy as jnp
from jax import lax
from jax.sharding import PartitionSpec as P

MAXDIL = 4
REACH = 2 * MAXDIL


def gather_projections(proj):
    axes = ("row", "col")
    count = lax.axis_size("row") * lax.axis_size("col")
    copies = jnp.broadcast_to(proj[None], (count,) + proj.shape)
    return lax.all_to_all(copies, axes, 0, 0, tiled=True).reshape(-1, proj.shape[1])


def inside(places, bins_total):
    return ((places >= 0) & (places < bins_total)).astype(jnp.float32)


def tap_groups(padded, weights, dilation):
    out_channels = weights.shape[1]
    in_channels = weights.shape[2]
    row_count = padded.shape[0] - 2 * MAXDIL
    col_count = padded.shape[1] - 2 * MAXDIL
    zero_index = jnp.zeros((), jnp.int32)
    pieces = []
    for tap in range(9):
        row_index = MAXDIL + (tap // 3 - 1) * dilation
        col_index = MAXDIL + (tap % 3 - 1) * dilation
        piece = lax.dynamic_slice(
            padded, (row_index, col_index, zero_index), (row_count, col_count, in_channels)
        )
        pieces.append(piece.reshape(row_count * col_count, in_channels))
    stacked = jnp.concatenate(pieces, axis=1)
    flat_weight = jnp.transpose(weights, (0, 2, 1)).reshape(9 * in_channels, out_channels)
    summed = jnp.dot(stacked, flat_weight, preferred_element_type=jnp.float32)
    return summed.reshape(row_count, col_count, out_channels)


def mirrored_taps(weights):
    return weights.reshape(3, 3, *weights.shape[1:]).swapaxes(0, 1).reshape(weights.shape)


def first_layer(every, taps, shift_bias, dilation, row_start, rows, col_start, cols):
    bins_total = every.shape[0]
    half = every.shape[1] // 2
    active = jnp.pad(jax.nn.relu(every), ((REACH, REACH), (0, 0)))
    row_part = jnp.einsum(
        "nk,tok->tno", active[:, :half], taps[:, :, :half], preferred_element_type=jnp.float32
    )
    col_part = jnp.einsum(
        "nk,tok->tno", active[:, half:], taps[:, :, half:], preferred_element_type=jnp.float32
    )
    span = bins_total + 2 * MAXDIL
    by_col, by_row = [], []
    for outer in range(3):
        along_rows = None
        along_cols = None
        for inner in range(3):
            piece_r = lax.dynamic_slice_in_dim(
                row_part[3 * inner + outer], MAXDIL + (inner - 1) * dilation, span, 0
            )
            piece_c = lax.dynamic_slice_in_dim(
                col_part[3 * outer + inner], MAXDIL + (inner - 1) * dilation, span, 0
            )
            along_rows = piece_r if along_rows is None else along_rows + piece_r
            along_cols = piece_c if along_cols is None else along_cols + piece_c
        by_col.append(along_rows)
        by_row.append(along_cols)

    def at(table, start, count):
        return lax.dynamic_slice_in_dim(table, start, count, 0)

    row_places = row_start - MAXDIL + jnp.arange(rows)
    col_places = col_start - MAXDIL + jnp.arange(cols)

    def conv_at(p_start, p_places, q_start, q_places, p_count, q_count, p_axis):
        total = None
        for step in range(3):
            q_in = inside(q_places + (step - 1) * dilation, bins_total)
            p_in = inside(p_places + (step - 1) * dilation, bins_total)
            term_p = at(by_col[step], p_start, p_count)
            term_q = at(by_row[step], q_start, q_count)
            if p_axis == 0:
                piece = term_p[:, None, :] * q_in[None, :, None] + term_q[None, :, :] * p_in[
                    :, None, None
                ]
            else:
                piece = term_p[None, :, :] * q_in[:, None, None] + term_q[:, None, :] * p_in[
                    None, :, None
                ]
            total = piece if total is None else total + piece
        return total

    padded = jnp.pad(every, ((MAXDIL, MAXDIL), (0, 0)))
    rows_here = at(padded, row_start, rows)
    cols_here = at(padded, col_start, cols)
    lower = jnp.arange(every.shape[1]) < half
    map0 = jnp.where(lower, rows_here[:, None, :], cols_here[None, :, :])
    map0_mirror = jnp.where(lower, cols_here[None, :, :], rows_here[:, None, :])
    bias = shift_bias[None, None, :]
    conv = conv_at(row_start, row_places, col_start, col_places, rows, cols, 0)
    conv_mirror = conv_at(col_start, col_places, row_start, row_places, cols, rows, 1)
    mixed = (map0.astype(jnp.float32) + bias + conv).astype(jnp.bfloat16)
    mixed_mirror = (map0_mirror.astype(jnp.float32) + bias + conv_mirror).astype(jnp.bfloat16)
    return mixed, mixed_mirror, row_places, col_places


def local(features, row_weight, col_weight, conv_weight, conv_bias, dilations):
    both = jnp.concatenate([row_weight, col_weight], axis=1)
    proj = jnp.dot(features, both, preferred_element_type=jnp.float32).astype(jnp.bfloat16)
    every = gather_projections(proj)
    bins_total = every.shape[0]
    row_size = bins_total // lax.axis_size("row")
    col_size = bins_total // lax.axis_size("col")
    row_start = lax.axis_index("row") * row_size
    col_start = lax.axis_index("col") * col_size
    rows1 = row_size + 2 * MAXDIL
    cols1 = col_size + 2 * MAXDIL

    mixed0, mixed0_mirror, row_places, col_places = first_layer(
        every, conv_weight[0], conv_bias[0], dilations[0], row_start, rows1, col_start, cols1
    )
    map1 = (0.5 * (mixed0.astype(jnp.float32) + mixed0_mirror.astype(jnp.float32))).astype(
        jnp.bfloat16
    )

    mask1 = (
        inside(row_places, bins_total)[:, None, None] * inside(col_places, bins_total)[None, :, None]
    ).astype(jnp.bfloat16)
    taps1 = jnp.concatenate([conv_weight[1], mirrored_taps(conv_weight[1])], axis=1)
    conv1 = tap_groups(jax.nn.relu(map1) * mask1, taps1, dilations[1])
    channels = conv_weight.shape[2]
    core = (slice(MAXDIL, MAXDIL + row_size), slice(MAXDIL, MAXDIL + col_size), slice(None))
    base1 = map1[core].astype(jnp.float32) + conv_bias[1][None, None, :]
    mixed1 = (base1 + conv1[:, :, :channels]).astype(jnp.bfloat16)
    mixed1_mirror = (base1 + conv1[:, :, channels:]).astype(jnp.bfloat16)
    pair = (0.5 * (mixed1.astype(jnp.float32) + mixed1_mirror.astype(jnp.float32))).astype(
        jnp.bfloat16
    )
    return jnp.transpose(pair, (2, 0, 1))


def solution(mesh):
    placed = (P(("row", "col"), None), P(), P(), P(), P(), P())
    return jax.shard_map(
        local, mesh=mesh, in_specs=placed, out_specs=P(None, "row", "col"), check_vma=False
    )
```

```python
import jax
import jax.numpy as jnp
from jax import lax
from jax.sharding import PartitionSpec as P

MAXDIL = 4
REACH = 2 * MAXDIL


def gather_projections(proj):
    axes = ("row", "col")
    count = lax.axis_size("row") * lax.axis_size("col")
    copies = jnp.broadcast_to(proj[None], (count,) + proj.shape)
    return lax.all_to_all(copies, axes, 0, 0, tiled=True).reshape(-1, proj.shape[1])


def inside(places, bins_total):
    return ((places >= 0) & (places < bins_total)).astype(jnp.float32)


def tap_groups(padded, weights, dilation):
    out_channels = weights.shape[1]
    in_channels = weights.shape[2]
    row_ext = padded.shape[0]
    row_count = row_ext - 2 * MAXDIL
    col_count = padded.shape[1] - 2 * MAXDIL
    zero_index = jnp.zeros((), jnp.int32)
    shifted = jnp.concatenate(
        [
            lax.dynamic_slice(
                padded,
                (zero_index, MAXDIL + (inner - 1) * dilation, zero_index),
                (row_ext, col_count, in_channels),
            )
            for inner in range(3)
        ],
        axis=2,
    )
    summed = None
    for outer in range(3):
        rows_now = lax.dynamic_slice_in_dim(shifted, MAXDIL + (outer - 1) * dilation, row_count, 0)
        group_weight = jnp.transpose(weights[3 * outer : 3 * outer + 3], (0, 2, 1)).reshape(
            3 * in_channels, out_channels
        )
        part = jnp.dot(
            rows_now.reshape(row_count * col_count, 3 * in_channels),
            group_weight,
            preferred_element_type=jnp.float32,
        )
        summed = part if summed is None else summed + part
    return summed.reshape(row_count, col_count, out_channels)


def mirrored_taps(weights):
    return weights.reshape(3, 3, *weights.shape[1:]).swapaxes(0, 1).reshape(weights.shape)


def first_layer(every, taps, shift_bias, dilation, row_start, rows, col_start, cols):
    bins_total = every.shape[0]
    half = every.shape[1] // 2
    active = jnp.pad(jax.nn.relu(every), ((REACH, REACH), (0, 0)))
    row_part = jnp.einsum(
        "nk,tok->tno", active[:, :half], taps[:, :, :half], preferred_element_type=jnp.float32
    )
    col_part = jnp.einsum(
        "nk,tok->tno", active[:, half:], taps[:, :, half:], preferred_element_type=jnp.float32
    )
    span = bins_total + 2 * MAXDIL
    by_col, by_row = [], []
    for outer in range(3):
        along_rows = None
        along_cols = None
        for inner in range(3):
            piece_r = lax.dynamic_slice_in_dim(
                row_part[3 * inner + outer], MAXDIL + (inner - 1) * dilation, span, 0
            )
            piece_c = lax.dynamic_slice_in_dim(
                col_part[3 * outer + inner], MAXDIL + (inner - 1) * dilation, span, 0
            )
            along_rows = piece_r if along_rows is None else along_rows + piece_r
            along_cols = piece_c if along_cols is None else along_cols + piece_c
        by_col.append(along_rows)
        by_row.append(along_cols)

    def at(table, start, count):
        return lax.dynamic_slice_in_dim(table, start, count, 0)

    row_places = row_start - MAXDIL + jnp.arange(rows)
    col_places = col_start - MAXDIL + jnp.arange(cols)

    padded = jnp.pad(every, ((MAXDIL, MAXDIL), (0, 0)))
    lower = jnp.arange(every.shape[1]) < half
    own_row = jnp.where(lower, padded, 0.0) + shift_bias[None, :]
    own_col = jnp.where(lower, 0.0, padded)
    row_tables = [
        own_row + by_col[1] + by_col[2],
        own_row + by_col[0] + by_col[1] + by_col[2],
        own_row + by_col[0] + by_col[1],
    ]
    col_tables = [
        own_col + by_row[1] + by_row[2],
        own_col + by_row[0] + by_row[1] + by_row[2],
        own_col + by_row[0] + by_row[1],
    ]

    def pick(tables, start, count, places, axis):
        low, mid, high = (at(table, start, count) for table in tables)
        shape = [1, 1, 1]
        shape[axis] = -1
        near_low = (places < dilation).reshape(shape)
        near_high = (places >= bins_total - dilation).reshape(shape)
        return jnp.where(near_low, low[:, None, :], jnp.where(near_high, high[:, None, :], mid[:, None, :])) if axis == 1 else jnp.where(
            near_low, low[None, :, :], jnp.where(near_high, high[None, :, :], mid[None, :, :])
        )

    mixed = (
        pick(row_tables, row_start, rows, col_places, 1)
        + pick(col_tables, col_start, cols, row_places, 0)
    ).astype(jnp.bfloat16)
    mixed_mirror = (
        pick(row_tables, col_start, cols, row_places, 0)
        + pick(col_tables, row_start, rows, col_places, 1)
    ).astype(jnp.bfloat16)
    return mixed, mixed_mirror, row_places, col_places


def local(features, row_weight, col_weight, conv_weight, conv_bias, dilations):
    both = jnp.concatenate([row_weight, col_weight], axis=1)
    proj = jnp.dot(features, both, preferred_element_type=jnp.float32).astype(jnp.bfloat16)
    every = gather_projections(proj)
    bins_total = every.shape[0]
    row_size = bins_total // lax.axis_size("row")
    col_size = bins_total // lax.axis_size("col")
    row_start = lax.axis_index("row") * row_size
    col_start = lax.axis_index("col") * col_size
    rows1 = row_size + 2 * MAXDIL
    cols1 = col_size + 2 * MAXDIL

    mixed0, mixed0_mirror, row_places, col_places = first_layer(
        every, conv_weight[0], conv_bias[0], dilations[0], row_start, rows1, col_start, cols1
    )
    map1 = (0.5 * (mixed0.astype(jnp.float32) + mixed0_mirror.astype(jnp.float32))).astype(
        jnp.bfloat16
    )

    mask1 = (
        inside(row_places, bins_total)[:, None, None] * inside(col_places, bins_total)[None, :, None]
    ).astype(jnp.bfloat16)
    taps1 = jnp.concatenate([conv_weight[1], mirrored_taps(conv_weight[1])], axis=1)
    conv1 = tap_groups(jax.nn.relu(map1) * mask1, taps1, dilations[1])
    channels = conv_weight.shape[2]
    core = (slice(MAXDIL, MAXDIL + row_size), slice(MAXDIL, MAXDIL + col_size), slice(None))
    base1 = map1[core].astype(jnp.float32) + conv_bias[1][None, None, :]
    mixed1 = (base1 + conv1[:, :, :channels]).astype(jnp.bfloat16)
    mixed1_mirror = (base1 + conv1[:, :, channels:]).astype(jnp.bfloat16)
    pair = (0.5 * (mixed1.astype(jnp.float32) + mixed1_mirror.astype(jnp.float32))).astype(
        jnp.bfloat16
    )
    return jnp.transpose(pair, (2, 0, 1))


def solution(mesh):
    placed = (P(("row", "col"), None), P(), P(), P(), P(), P())
    return jax.shard_map(
        local, mesh=mesh, in_specs=placed, out_specs=P(None, "row", "col"), check_vma=False
    )
```

```python
import jax
import jax.numpy as jnp
from jax import lax
from jax.sharding import PartitionSpec as P

MAXDIL = 4
REACH = 2 * MAXDIL


def gather_projections(proj):
    axes = ("row", "col")
    count = lax.axis_size("row") * lax.axis_size("col")
    copies = jnp.broadcast_to(proj[None], (count,) + proj.shape)
    return lax.all_to_all(copies, axes, 0, 0, tiled=True).reshape(-1, proj.shape[1])


def inside(places, bins_total):
    return ((places >= 0) & (places < bins_total)).astype(jnp.float32)


def tap_groups(padded, weights, dilation):
    out_channels = weights.shape[1]
    in_channels = weights.shape[2]
    row_count = padded.shape[0] - 2 * MAXDIL
    col_count = padded.shape[1] - 2 * MAXDIL
    zero_index = jnp.zeros((), jnp.int32)
    pieces = []
    for tap in range(9):
        row_index = MAXDIL + (tap // 3 - 1) * dilation
        col_index = MAXDIL + (tap % 3 - 1) * dilation
        piece = lax.dynamic_slice(
            padded, (row_index, col_index, zero_index), (row_count, col_count, in_channels)
        )
        pieces.append(piece.reshape(row_count * col_count, in_channels))
    stacked = jnp.concatenate(pieces, axis=1)
    flat_weight = jnp.transpose(weights, (0, 2, 1)).reshape(9 * in_channels, out_channels)
    summed = jnp.dot(stacked, flat_weight, preferred_element_type=jnp.float32)
    return summed.reshape(row_count, col_count, out_channels)


def mirrored_taps(weights):
    return weights.reshape(3, 3, *weights.shape[1:]).swapaxes(0, 1).reshape(weights.shape)


def first_layer(every, taps, shift_bias, dilation, row_start, rows, col_start, cols):
    bins_total = every.shape[0]
    half = every.shape[1] // 2
    active = jnp.pad(jax.nn.relu(every), ((REACH, REACH), (0, 0)))
    row_part = jnp.einsum(
        "nk,tok->tno", active[:, :half], taps[:, :, :half], preferred_element_type=jnp.float32
    )
    col_part = jnp.einsum(
        "nk,tok->tno", active[:, half:], taps[:, :, half:], preferred_element_type=jnp.float32
    )
    span = bins_total + 2 * MAXDIL
    by_col, by_row = [], []
    for outer in range(3):
        along_rows = None
        along_cols = None
        for inner in range(3):
            piece_r = lax.dynamic_slice_in_dim(
                row_part[3 * inner + outer], MAXDIL + (inner - 1) * dilation, span, 0
            )
            piece_c = lax.dynamic_slice_in_dim(
                col_part[3 * outer + inner], MAXDIL + (inner - 1) * dilation, span, 0
            )
            along_rows = piece_r if along_rows is None else along_rows + piece_r
            along_cols = piece_c if along_cols is None else along_cols + piece_c
        by_col.append(along_rows)
        by_row.append(along_cols)

    def at(table, start, count):
        return lax.dynamic_slice_in_dim(table, start, count, 0)

    row_places = row_start - MAXDIL + jnp.arange(rows)
    col_places = col_start - MAXDIL + jnp.arange(cols)

    padded = jnp.pad(every, ((MAXDIL, MAXDIL), (0, 0)))
    lower = jnp.arange(every.shape[1]) < half
    own_row = jnp.where(lower, padded, 0.0) + shift_bias[None, :]
    own_col = jnp.where(lower, 0.0, padded)
    row_tables = [
        own_row + by_col[1] + by_col[2],
        own_row + by_col[0] + by_col[1] + by_col[2],
        own_row + by_col[0] + by_col[1],
    ]
    col_tables = [
        own_col + by_row[1] + by_row[2],
        own_col + by_row[0] + by_row[1] + by_row[2],
        own_col + by_row[0] + by_row[1],
    ]

    def pick(tables, start, count, places, axis):
        low, mid, high = (at(table, start, count) for table in tables)
        shape = [1, 1, 1]
        shape[axis] = -1
        near_low = (places < dilation).reshape(shape)
        near_high = (places >= bins_total - dilation).reshape(shape)
        return jnp.where(near_low, low[:, None, :], jnp.where(near_high, high[:, None, :], mid[:, None, :])) if axis == 1 else jnp.where(
            near_low, low[None, :, :], jnp.where(near_high, high[None, :, :], mid[None, :, :])
        )

    mixed = (
        pick(row_tables, row_start, rows, col_places, 1)
        + pick(col_tables, col_start, cols, row_places, 0)
    ).astype(jnp.bfloat16)
    mixed_mirror = (
        pick(row_tables, col_start, cols, row_places, 0)
        + pick(col_tables, row_start, rows, col_places, 1)
    ).astype(jnp.bfloat16)
    return mixed, mixed_mirror, row_places, col_places


def local(features, row_weight, col_weight, conv_weight, conv_bias, dilations):
    both = jnp.concatenate([row_weight, col_weight], axis=1)
    proj = jnp.dot(features, both, preferred_element_type=jnp.float32).astype(jnp.bfloat16)
    every = gather_projections(proj)
    bins_total = every.shape[0]
    row_size = bins_total // lax.axis_size("row")
    col_size = bins_total // lax.axis_size("col")
    row_start = lax.axis_index("row") * row_size
    col_start = lax.axis_index("col") * col_size
    rows1 = row_size + 2 * MAXDIL
    cols1 = col_size + 2 * MAXDIL

    mixed0, mixed0_mirror, row_places, col_places = first_layer(
        every, conv_weight[0], conv_bias[0], dilations[0], row_start, rows1, col_start, cols1
    )
    map1 = (0.5 * (mixed0.astype(jnp.float32) + mixed0_mirror.astype(jnp.float32))).astype(
        jnp.bfloat16
    )

    mask1 = (
        inside(row_places, bins_total)[:, None, None] * inside(col_places, bins_total)[None, :, None]
    ).astype(jnp.bfloat16)
    taps1 = jnp.concatenate([conv_weight[1], mirrored_taps(conv_weight[1])], axis=1)
    conv1 = tap_groups(jax.nn.relu(map1) * mask1, taps1, dilations[1])
    channels = conv_weight.shape[2]
    core = (slice(MAXDIL, MAXDIL + row_size), slice(MAXDIL, MAXDIL + col_size), slice(None))
    base1 = map1[core].astype(jnp.float32) + conv_bias[1][None, None, :]
    mixed1 = (base1 + conv1[:, :, :channels]).astype(jnp.bfloat16)
    mixed1_mirror = (base1 + conv1[:, :, channels:]).astype(jnp.bfloat16)
    pair = (0.5 * (mixed1.astype(jnp.float32) + mixed1_mirror.astype(jnp.float32))).astype(
        jnp.bfloat16
    )
    return jnp.transpose(pair, (2, 0, 1))


def solution(mesh):
    placed = (P(("row", "col"), None), P(), P(), P(), P(), P())
    return jax.shard_map(
        local, mesh=mesh, in_specs=placed, out_specs=P(None, "row", "col"), check_vma=False
    )
```

```python
import jax
import jax.numpy as jnp
from jax import lax
from jax.sharding import PartitionSpec as P

MAXDIL = 4
REACH = 2 * MAXDIL


def gather_projections(proj):
    axes = ("row", "col")
    count = lax.axis_size("row") * lax.axis_size("col")
    copies = jnp.broadcast_to(proj[None], (count,) + proj.shape)
    return lax.all_to_all(copies, axes, 0, 0, tiled=True).reshape(-1, proj.shape[1])


def inside(places, bins_total):
    return ((places >= 0) & (places < bins_total)).astype(jnp.float32)


def tap_groups(padded, weights, dilation):
    out_channels = weights.shape[1]
    in_channels = weights.shape[2]
    row_count = padded.shape[0] - 2 * MAXDIL
    col_count = padded.shape[1] - 2 * MAXDIL
    zero_index = jnp.zeros((), jnp.int32)
    pieces = []
    for tap in range(9):
        row_index = MAXDIL + (tap // 3 - 1) * dilation
        col_index = MAXDIL + (tap % 3 - 1) * dilation
        piece = lax.dynamic_slice(
            padded, (row_index, col_index, zero_index), (row_count, col_count, in_channels)
        )
        pieces.append(piece.reshape(row_count * col_count, in_channels))
    stacked = jnp.concatenate(pieces, axis=1)
    flat_weight = jnp.transpose(weights, (0, 2, 1)).reshape(9 * in_channels, out_channels)
    summed = jnp.dot(stacked, flat_weight, preferred_element_type=jnp.float32)
    return summed.reshape(row_count, col_count, out_channels)


def native_conv(act, weights, dilation, rows, cols):
    kernel = jnp.transpose(weights.reshape(3, 3, *weights.shape[1:]), (0, 1, 3, 2))

    def branch(d):
        def run(x, w):
            lo = MAXDIL - d
            piece = x[lo : lo + rows + 2 * d, lo : lo + cols + 2 * d, :]
            return lax.conv_general_dilated(
                piece[None],
                w,
                window_strides=(1, 1),
                padding="VALID",
                rhs_dilation=(d, d),
                dimension_numbers=("NHWC", "HWIO", "NHWC"),
                preferred_element_type=jnp.float32,
            )[0]

        return run

    return lax.switch(dilation - 1, [branch(d) for d in range(1, MAXDIL + 1)], act, kernel)


def mirrored_taps(weights):
    return weights.reshape(3, 3, *weights.shape[1:]).swapaxes(0, 1).reshape(weights.shape)


def first_layer(every, taps, shift_bias, dilation, row_start, rows, col_start, cols):
    bins_total = every.shape[0]
    half = every.shape[1] // 2
    active = jnp.pad(jax.nn.relu(every), ((REACH, REACH), (0, 0)))
    row_part = jnp.einsum(
        "nk,tok->tno", active[:, :half], taps[:, :, :half], preferred_element_type=jnp.float32
    )
    col_part = jnp.einsum(
        "nk,tok->tno", active[:, half:], taps[:, :, half:], preferred_element_type=jnp.float32
    )
    span = bins_total + 2 * MAXDIL
    by_col, by_row = [], []
    for outer in range(3):
        along_rows = None
        along_cols = None
        for inner in range(3):
            piece_r = lax.dynamic_slice_in_dim(
                row_part[3 * inner + outer], MAXDIL + (inner - 1) * dilation, span, 0
            )
            piece_c = lax.dynamic_slice_in_dim(
                col_part[3 * outer + inner], MAXDIL + (inner - 1) * dilation, span, 0
            )
            along_rows = piece_r if along_rows is None else along_rows + piece_r
            along_cols = piece_c if along_cols is None else along_cols + piece_c
        by_col.append(along_rows)
        by_row.append(along_cols)

    def at(table, start, count):
        return lax.dynamic_slice_in_dim(table, start, count, 0)

    row_places = row_start - MAXDIL + jnp.arange(rows)
    col_places = col_start - MAXDIL + jnp.arange(cols)

    padded = jnp.pad(every, ((MAXDIL, MAXDIL), (0, 0)))
    lower = jnp.arange(every.shape[1]) < half
    own_row = jnp.where(lower, padded, 0.0) + shift_bias[None, :]
    own_col = jnp.where(lower, 0.0, padded)
    row_tables = [
        own_row + by_col[1] + by_col[2],
        own_row + by_col[0] + by_col[1] + by_col[2],
        own_row + by_col[0] + by_col[1],
    ]
    col_tables = [
        own_col + by_row[1] + by_row[2],
        own_col + by_row[0] + by_row[1] + by_row[2],
        own_col + by_row[0] + by_row[1],
    ]

    def pick(tables, start, count, places, axis):
        low, mid, high = (at(table, start, count) for table in tables)
        shape = [1, 1, 1]
        shape[axis] = -1
        near_low = (places < dilation).reshape(shape)
        near_high = (places >= bins_total - dilation).reshape(shape)
        return jnp.where(near_low, low[:, None, :], jnp.where(near_high, high[:, None, :], mid[:, None, :])) if axis == 1 else jnp.where(
            near_low, low[None, :, :], jnp.where(near_high, high[None, :, :], mid[None, :, :])
        )

    mixed = (
        pick(row_tables, row_start, rows, col_places, 1)
        + pick(col_tables, col_start, cols, row_places, 0)
    ).astype(jnp.bfloat16)
    mixed_mirror = (
        pick(row_tables, col_start, cols, row_places, 0)
        + pick(col_tables, row_start, rows, col_places, 1)
    ).astype(jnp.bfloat16)
    return mixed, mixed_mirror, row_places, col_places


def local(features, row_weight, col_weight, conv_weight, conv_bias, dilations):
    both = jnp.concatenate([row_weight, col_weight], axis=1)
    proj = jnp.dot(features, both, preferred_element_type=jnp.float32).astype(jnp.bfloat16)
    every = gather_projections(proj)
    bins_total = every.shape[0]
    row_size = bins_total // lax.axis_size("row")
    col_size = bins_total // lax.axis_size("col")
    row_start = lax.axis_index("row") * row_size
    col_start = lax.axis_index("col") * col_size
    rows1 = row_size + 2 * MAXDIL
    cols1 = col_size + 2 * MAXDIL

    mixed0, mixed0_mirror, row_places, col_places = first_layer(
        every, conv_weight[0], conv_bias[0], dilations[0], row_start, rows1, col_start, cols1
    )
    map1 = (0.5 * (mixed0.astype(jnp.float32) + mixed0_mirror.astype(jnp.float32))).astype(
        jnp.bfloat16
    )

    mask1 = (
        inside(row_places, bins_total)[:, None, None] * inside(col_places, bins_total)[None, :, None]
    ).astype(jnp.bfloat16)
    taps1 = jnp.concatenate([conv_weight[1], mirrored_taps(conv_weight[1])], axis=1)
    conv1 = native_conv(jax.nn.relu(map1) * mask1, taps1, dilations[1], row_size, col_size)
    channels = conv_weight.shape[2]
    core = (slice(MAXDIL, MAXDIL + row_size), slice(MAXDIL, MAXDIL + col_size), slice(None))
    base1 = map1[core].astype(jnp.float32) + conv_bias[1][None, None, :]
    mixed1 = (base1 + conv1[:, :, :channels]).astype(jnp.bfloat16)
    mixed1_mirror = (base1 + conv1[:, :, channels:]).astype(jnp.bfloat16)
    pair = (0.5 * (mixed1.astype(jnp.float32) + mixed1_mirror.astype(jnp.float32))).astype(
        jnp.bfloat16
    )
    return jnp.transpose(pair, (2, 0, 1))


def solution(mesh):
    placed = (P(("row", "col"), None), P(), P(), P(), P(), P())
    return jax.shard_map(
        local, mesh=mesh, in_specs=placed, out_specs=P(None, "row", "col"), check_vma=False
    )
```

```python
import jax
import jax.numpy as jnp
from jax import lax
from jax.sharding import PartitionSpec as P

MAXDIL = 4
REACH = 2 * MAXDIL


def gather_projections(proj):
    axes = ("row", "col")
    count = lax.axis_size("row") * lax.axis_size("col")
    copies = jnp.broadcast_to(proj[None], (count,) + proj.shape)
    return lax.all_to_all(copies, axes, 0, 0, tiled=True).reshape(-1, proj.shape[1])


def inside(places, bins_total):
    return ((places >= 0) & (places < bins_total)).astype(jnp.float32)


def tap_groups(padded, weights, dilation):
    out_channels = weights.shape[1]
    in_channels = weights.shape[2]
    row_count = padded.shape[0] - 2 * MAXDIL
    col_count = padded.shape[1] - 2 * MAXDIL
    zero_index = jnp.zeros((), jnp.int32)
    pieces = []
    for tap in range(9):
        row_index = MAXDIL + (tap // 3 - 1) * dilation
        col_index = MAXDIL + (tap % 3 - 1) * dilation
        piece = lax.dynamic_slice(
            padded, (row_index, col_index, zero_index), (row_count, col_count, in_channels)
        )
        pieces.append(piece.reshape(row_count * col_count, in_channels))
    stacked = jnp.concatenate(pieces, axis=1)
    flat_weight = jnp.transpose(weights, (0, 2, 1)).reshape(9 * in_channels, out_channels)
    summed = jnp.dot(stacked, flat_weight, preferred_element_type=jnp.float32)
    return summed.reshape(row_count, col_count, out_channels)


def mirrored_taps(weights):
    return weights.reshape(3, 3, *weights.shape[1:]).swapaxes(0, 1).reshape(weights.shape)


def first_layer(every, taps, shift_bias, dilation, row_start, rows, col_start, cols):
    bins_total = every.shape[0]
    half = every.shape[1] // 2
    lower = jnp.arange(every.shape[1]) < half
    active = jnp.pad(jax.nn.relu(every), ((REACH, REACH), (0, 0)))
    padded = jnp.pad(every, ((MAXDIL, MAXDIL), (0, 0)))

    def tables(start, count):
        window = lax.dynamic_slice_in_dim(active, start, count + 2 * MAXDIL, 0)
        row_part = jnp.einsum(
            "nk,tok->tno", window[:, :half], taps[:, :, :half], preferred_element_type=jnp.float32
        )
        col_part = jnp.einsum(
            "nk,tok->tno", window[:, half:], taps[:, :, half:], preferred_element_type=jnp.float32
        )
        by_col, by_row = [], []
        for outer in range(3):
            along_rows = None
            along_cols = None
            for inner in range(3):
                piece_r = lax.dynamic_slice_in_dim(
                    row_part[3 * inner + outer], MAXDIL + (inner - 1) * dilation, count, 0
                )
                piece_c = lax.dynamic_slice_in_dim(
                    col_part[3 * outer + inner], MAXDIL + (inner - 1) * dilation, count, 0
                )
                along_rows = piece_r if along_rows is None else along_rows + piece_r
                along_cols = piece_c if along_cols is None else along_cols + piece_c
            by_col.append(along_rows)
            by_row.append(along_cols)
        own = lax.dynamic_slice_in_dim(padded, start, count, 0)
        own_row = jnp.where(lower, own, 0.0) + shift_bias[None, :]
        own_col = jnp.where(lower, 0.0, own)
        row_tables = [
            own_row + by_col[1] + by_col[2],
            own_row + by_col[0] + by_col[1] + by_col[2],
            own_row + by_col[0] + by_col[1],
        ]
        col_tables = [
            own_col + by_row[1] + by_row[2],
            own_col + by_row[0] + by_row[1] + by_row[2],
            own_col + by_row[0] + by_row[1],
        ]
        return row_tables, col_tables

    row_places = row_start - MAXDIL + jnp.arange(rows)
    col_places = col_start - MAXDIL + jnp.arange(cols)
    rows_row_tables, rows_col_tables = tables(row_start, rows)
    cols_row_tables, cols_col_tables = tables(col_start, cols)

    def pick(tables_here, places, axis):
        low, mid, high = tables_here
        shape = [1, 1, 1]
        shape[axis] = -1
        near_low = (places < dilation).reshape(shape)
        near_high = (places >= bins_total - dilation).reshape(shape)
        if axis == 1:
            low, mid, high = low[:, None, :], mid[:, None, :], high[:, None, :]
        else:
            low, mid, high = low[None, :, :], mid[None, :, :], high[None, :, :]
        return jnp.where(near_low, low, jnp.where(near_high, high, mid))

    mixed = (
        pick(rows_row_tables, col_places, 1) + pick(cols_col_tables, row_places, 0)
    ).astype(jnp.bfloat16)
    mixed_mirror = (
        pick(cols_row_tables, row_places, 0) + pick(rows_col_tables, col_places, 1)
    ).astype(jnp.bfloat16)
    return mixed, mixed_mirror, row_places, col_places


def local(features, row_weight, col_weight, conv_weight, conv_bias, dilations):
    both = jnp.concatenate([row_weight, col_weight], axis=1)
    proj = jnp.dot(features, both, preferred_element_type=jnp.float32).astype(jnp.bfloat16)
    every = gather_projections(proj)
    bins_total = every.shape[0]
    row_size = bins_total // lax.axis_size("row")
    col_size = bins_total // lax.axis_size("col")
    row_start = lax.axis_index("row") * row_size
    col_start = lax.axis_index("col") * col_size
    rows1 = row_size + 2 * MAXDIL
    cols1 = col_size + 2 * MAXDIL

    mixed0, mixed0_mirror, row_places, col_places = first_layer(
        every, conv_weight[0], conv_bias[0], dilations[0], row_start, rows1, col_start, cols1
    )
    map1 = (0.5 * (mixed0.astype(jnp.float32) + mixed0_mirror.astype(jnp.float32))).astype(
        jnp.bfloat16
    )

    mask1 = (
        inside(row_places, bins_total)[:, None, None] * inside(col_places, bins_total)[None, :, None]
    ).astype(jnp.bfloat16)
    taps1 = jnp.concatenate([conv_weight[1], mirrored_taps(conv_weight[1])], axis=1)
    conv1 = tap_groups(jax.nn.relu(map1) * mask1, taps1, dilations[1])
    channels = conv_weight.shape[2]
    core = (slice(MAXDIL, MAXDIL + row_size), slice(MAXDIL, MAXDIL + col_size), slice(None))
    base1 = map1[core].astype(jnp.float32) + conv_bias[1][None, None, :]
    mixed1 = (base1 + conv1[:, :, :channels]).astype(jnp.bfloat16)
    mixed1_mirror = (base1 + conv1[:, :, channels:]).astype(jnp.bfloat16)
    pair = (0.5 * (mixed1.astype(jnp.float32) + mixed1_mirror.astype(jnp.float32))).astype(
        jnp.bfloat16
    )
    return jnp.transpose(pair, (2, 0, 1))


def solution(mesh):
    placed = (P(("row", "col"), None), P(), P(), P(), P(), P())
    return jax.shard_map(
        local, mesh=mesh, in_specs=placed, out_specs=P(None, "row", "col"), check_vma=False
    )
```

```python
import jax
import jax.numpy as jnp
from jax import lax
from jax.sharding import PartitionSpec as P

MAXDIL = 4
REACH = 2 * MAXDIL


def gather_projections(proj):
    axes = ("row", "col")
    count = lax.axis_size("row") * lax.axis_size("col")
    copies = jnp.broadcast_to(proj[None], (count,) + proj.shape)
    return lax.all_to_all(copies, axes, 0, 0, tiled=True).reshape(-1, proj.shape[1])


def inside(places, bins_total):
    return ((places >= 0) & (places < bins_total)).astype(jnp.float32)


def tap_groups(padded, weights, dilation):
    out_channels = weights.shape[1]
    in_channels = weights.shape[2]
    row_count = padded.shape[0] - 2 * MAXDIL
    col_count = padded.shape[1] - 2 * MAXDIL
    zero_index = jnp.zeros((), jnp.int32)
    pieces = []
    for tap in range(9):
        row_index = MAXDIL + (tap // 3 - 1) * dilation
        col_index = MAXDIL + (tap % 3 - 1) * dilation
        piece = lax.dynamic_slice(
            padded, (row_index, col_index, zero_index), (row_count, col_count, in_channels)
        )
        pieces.append(piece.reshape(row_count * col_count, in_channels))
    stacked = jnp.concatenate(pieces, axis=1)
    flat_weight = jnp.transpose(weights, (0, 2, 1)).reshape(9 * in_channels, out_channels)
    summed = jnp.dot(stacked, flat_weight, preferred_element_type=jnp.float32)
    return summed.reshape(row_count, col_count, out_channels)


def mirrored_taps(weights):
    return weights.reshape(3, 3, *weights.shape[1:]).swapaxes(0, 1).reshape(weights.shape)


def packed_rows(places, channels):
    return jnp.repeat(places.reshape(-1, 2), channels, axis=1)[:, None, :]


def unpack(packed, channels):
    halves, cols = packed.shape[0], packed.shape[1]
    split = packed.reshape(halves, cols, 2, channels)
    return jnp.transpose(split, (0, 2, 1, 3)).reshape(2 * halves, cols, channels)


def first_layer(every, taps, shift_bias, dilation, row_start, rows, col_start, cols):
    bins_total = every.shape[0]
    half = every.shape[1] // 2
    lower = jnp.arange(every.shape[1]) < half
    active = jnp.pad(jax.nn.relu(every), ((REACH, REACH), (0, 0)))
    padded = jnp.pad(every, ((MAXDIL, MAXDIL), (0, 0)))

    def tables(start, count):
        window = lax.dynamic_slice_in_dim(active, start, count + 2 * MAXDIL, 0)
        row_part = jnp.einsum(
            "nk,tok->tno", window[:, :half], taps[:, :, :half], preferred_element_type=jnp.float32
        )
        col_part = jnp.einsum(
            "nk,tok->tno", window[:, half:], taps[:, :, half:], preferred_element_type=jnp.float32
        )
        by_col, by_row = [], []
        for outer in range(3):
            along_rows = None
            along_cols = None
            for inner in range(3):
                piece_r = lax.dynamic_slice_in_dim(
                    row_part[3 * inner + outer], MAXDIL + (inner - 1) * dilation, count, 0
                )
                piece_c = lax.dynamic_slice_in_dim(
                    col_part[3 * outer + inner], MAXDIL + (inner - 1) * dilation, count, 0
                )
                along_rows = piece_r if along_rows is None else along_rows + piece_r
                along_cols = piece_c if along_cols is None else along_cols + piece_c
            by_col.append(along_rows)
            by_row.append(along_cols)
        own = lax.dynamic_slice_in_dim(padded, start, count, 0)
        own_row = jnp.where(lower, own, 0.0) + shift_bias[None, :]
        own_col = jnp.where(lower, 0.0, own)
        row_tables = [
            own_row + by_col[1] + by_col[2],
            own_row + by_col[0] + by_col[1] + by_col[2],
            own_row + by_col[0] + by_col[1],
        ]
        col_tables = [
            own_col + by_row[1] + by_row[2],
            own_col + by_row[0] + by_row[1] + by_row[2],
            own_col + by_row[0] + by_row[1],
        ]
        return row_tables, col_tables

    row_places = row_start - MAXDIL + jnp.arange(rows)
    col_places = col_start - MAXDIL + jnp.arange(cols)
    rows_row_tables, rows_col_tables = tables(row_start, rows)
    cols_row_tables, cols_col_tables = tables(col_start, cols)

    def over_rows(table):
        return table.reshape(rows // 2, 1, 2 * table.shape[1])

    def over_cols(table):
        return jnp.concatenate([table, table], axis=1)[None]

    def pick(tables_here, along_rows, class_places):
        low, mid, high = (over_rows(t) if along_rows else over_cols(t) for t in tables_here)
        return jnp.where(
            class_places < dilation,
            low,
            jnp.where(class_places >= bins_total - dilation, high, mid),
        )

    row_class = packed_rows(row_places, every.shape[1])
    col_class = col_places[None, :, None]
    mixed = (
        pick(rows_row_tables, True, col_class) + pick(cols_col_tables, False, row_class)
    ).astype(jnp.bfloat16)
    mixed_mirror = (
        pick(cols_row_tables, False, row_class) + pick(rows_col_tables, True, col_class)
    ).astype(jnp.bfloat16)
    return mixed, mixed_mirror, row_places, col_places


def local(features, row_weight, col_weight, conv_weight, conv_bias, dilations):
    both = jnp.concatenate([row_weight, col_weight], axis=1)
    proj = jnp.dot(features, both, preferred_element_type=jnp.float32).astype(jnp.bfloat16)
    every = gather_projections(proj)
    bins_total = every.shape[0]
    row_size = bins_total // lax.axis_size("row")
    col_size = bins_total // lax.axis_size("col")
    row_start = lax.axis_index("row") * row_size
    col_start = lax.axis_index("col") * col_size
    rows1 = row_size + 2 * MAXDIL
    cols1 = col_size + 2 * MAXDIL

    mixed0, mixed0_mirror, row_places, col_places = first_layer(
        every, conv_weight[0], conv_bias[0], dilations[0], row_start, rows1, col_start, cols1
    )
    map1 = (0.5 * (mixed0.astype(jnp.float32) + mixed0_mirror.astype(jnp.float32))).astype(
        jnp.bfloat16
    )

    channels = conv_weight.shape[2]
    mask1 = (
        inside(packed_rows(row_places, channels), bins_total)
        * inside(col_places, bins_total)[None, :, None]
    ).astype(jnp.bfloat16)
    taps1 = jnp.concatenate([conv_weight[1], mirrored_taps(conv_weight[1])], axis=1)
    conv1 = tap_groups(unpack(jax.nn.relu(map1) * mask1, channels), taps1, dilations[1])
    core = (slice(MAXDIL, MAXDIL + row_size), slice(MAXDIL, MAXDIL + col_size), slice(None))
    base1 = unpack(map1, channels)[core].astype(jnp.float32) + conv_bias[1][None, None, :]
    mixed1 = (base1 + conv1[:, :, :channels]).astype(jnp.bfloat16)
    mixed1_mirror = (base1 + conv1[:, :, channels:]).astype(jnp.bfloat16)
    pair = (0.5 * (mixed1.astype(jnp.float32) + mixed1_mirror.astype(jnp.float32))).astype(
        jnp.bfloat16
    )
    return jnp.transpose(pair, (2, 0, 1))


def solution(mesh):
    placed = (P(("row", "col"), None), P(), P(), P(), P(), P())
    return jax.shard_map(
        local, mesh=mesh, in_specs=placed, out_specs=P(None, "row", "col"), check_vma=False
    )
```

```python
import jax
import jax.numpy as jnp
from jax import lax
from jax.sharding import PartitionSpec as P

MAXDIL = 4
REACH = 2 * MAXDIL


def gather_projections(proj):
    axes = ("row", "col")
    count = lax.axis_size("row") * lax.axis_size("col")
    flat = proj.reshape(2, -1)
    copies = jnp.broadcast_to(flat[None], (count,) + flat.shape)
    return lax.all_to_all(copies, axes, 0, 0, tiled=True).reshape(-1, proj.shape[1])


def inside(places, bins_total):
    return ((places >= 0) & (places < bins_total)).astype(jnp.float32)


def tap_groups(padded, weights, dilation):
    out_channels = weights.shape[1]
    in_channels = weights.shape[2]
    row_count = padded.shape[0] - 2 * MAXDIL
    col_count = padded.shape[1] - 2 * MAXDIL
    zero_index = jnp.zeros((), jnp.int32)
    pieces = []
    for tap in range(9):
        row_index = MAXDIL + (tap // 3 - 1) * dilation
        col_index = MAXDIL + (tap % 3 - 1) * dilation
        piece = lax.dynamic_slice(
            padded, (row_index, col_index, zero_index), (row_count, col_count, in_channels)
        )
        pieces.append(piece.reshape(row_count * col_count, in_channels))
    stacked = jnp.concatenate(pieces, axis=1)
    flat_weight = jnp.transpose(weights, (0, 2, 1)).reshape(9 * in_channels, out_channels)
    summed = jnp.dot(stacked, flat_weight, preferred_element_type=jnp.float32)
    return summed.reshape(row_count, col_count, out_channels)


def mirrored_taps(weights):
    return weights.reshape(3, 3, *weights.shape[1:]).swapaxes(0, 1).reshape(weights.shape)


def first_layer(every, taps, shift_bias, dilation, row_start, rows, col_start, cols):
    bins_total = every.shape[0]
    half = every.shape[1] // 2
    lower = jnp.arange(every.shape[1]) < half
    active = jnp.pad(jax.nn.relu(every), ((REACH, REACH), (0, 0)))
    padded = jnp.pad(every, ((MAXDIL, MAXDIL), (0, 0)))

    def tables(start, count):
        window = lax.dynamic_slice_in_dim(active, start, count + 2 * MAXDIL, 0)
        row_part = jnp.einsum(
            "nk,tok->tno", window[:, :half], taps[:, :, :half], preferred_element_type=jnp.float32
        )
        col_part = jnp.einsum(
            "nk,tok->tno", window[:, half:], taps[:, :, half:], preferred_element_type=jnp.float32
        )
        by_col, by_row = [], []
        for outer in range(3):
            along_rows = None
            along_cols = None
            for inner in range(3):
                piece_r = lax.dynamic_slice_in_dim(
                    row_part[3 * inner + outer], MAXDIL + (inner - 1) * dilation, count, 0
                )
                piece_c = lax.dynamic_slice_in_dim(
                    col_part[3 * outer + inner], MAXDIL + (inner - 1) * dilation, count, 0
                )
                along_rows = piece_r if along_rows is None else along_rows + piece_r
                along_cols = piece_c if along_cols is None else along_cols + piece_c
            by_col.append(along_rows)
            by_row.append(along_cols)
        own = lax.dynamic_slice_in_dim(padded, start, count, 0)
        own_row = jnp.where(lower, own, 0.0) + shift_bias[None, :]
        own_col = jnp.where(lower, 0.0, own)
        row_tables = [
            own_row + by_col[1] + by_col[2],
            own_row + by_col[0] + by_col[1] + by_col[2],
            own_row + by_col[0] + by_col[1],
        ]
        col_tables = [
            own_col + by_row[1] + by_row[2],
            own_col + by_row[0] + by_row[1] + by_row[2],
            own_col + by_row[0] + by_row[1],
        ]
        return row_tables, col_tables

    row_places = row_start - MAXDIL + jnp.arange(rows)
    col_places = col_start - MAXDIL + jnp.arange(cols)
    rows_row_tables, rows_col_tables = tables(row_start, rows)
    cols_row_tables, cols_col_tables = tables(col_start, cols)

    def pick(tables_here, places, axis):
        low, mid, high = tables_here
        shape = [1, 1, 1]
        shape[axis] = -1
        near_low = (places < dilation).reshape(shape)
        near_high = (places >= bins_total - dilation).reshape(shape)
        if axis == 1:
            low, mid, high = low[:, None, :], mid[:, None, :], high[:, None, :]
        else:
            low, mid, high = low[None, :, :], mid[None, :, :], high[None, :, :]
        return jnp.where(near_low, low, jnp.where(near_high, high, mid))

    mixed = (
        pick(rows_row_tables, col_places, 1) + pick(cols_col_tables, row_places, 0)
    ).astype(jnp.bfloat16)
    mixed_mirror = (
        pick(cols_row_tables, row_places, 0) + pick(rows_col_tables, col_places, 1)
    ).astype(jnp.bfloat16)
    return mixed, mixed_mirror, row_places, col_places


def local(features, row_weight, col_weight, conv_weight, conv_bias, dilations):
    both = jnp.concatenate([row_weight, col_weight], axis=1)
    proj = jnp.dot(features, both, preferred_element_type=jnp.float32).astype(jnp.bfloat16)
    every = gather_projections(proj)
    bins_total = every.shape[0]
    row_size = bins_total // lax.axis_size("row")
    col_size = bins_total // lax.axis_size("col")
    row_start = lax.axis_index("row") * row_size
    col_start = lax.axis_index("col") * col_size
    rows1 = row_size + 2 * MAXDIL
    cols1 = col_size + 2 * MAXDIL

    mixed0, mixed0_mirror, row_places, col_places = first_layer(
        every, conv_weight[0], conv_bias[0], dilations[0], row_start, rows1, col_start, cols1
    )
    map1 = (0.5 * (mixed0.astype(jnp.float32) + mixed0_mirror.astype(jnp.float32))).astype(
        jnp.bfloat16
    )

    mask1 = (
        inside(row_places, bins_total)[:, None, None] * inside(col_places, bins_total)[None, :, None]
    ).astype(jnp.bfloat16)
    taps1 = jnp.concatenate([conv_weight[1], mirrored_taps(conv_weight[1])], axis=1)
    conv1 = tap_groups(jax.nn.relu(map1) * mask1, taps1, dilations[1])
    channels = conv_weight.shape[2]
    core = (slice(MAXDIL, MAXDIL + row_size), slice(MAXDIL, MAXDIL + col_size), slice(None))
    base1 = map1[core].astype(jnp.float32) + conv_bias[1][None, None, :]
    mixed1 = (base1 + conv1[:, :, :channels]).astype(jnp.bfloat16)
    mixed1_mirror = (base1 + conv1[:, :, channels:]).astype(jnp.bfloat16)
    pair = (0.5 * (mixed1.astype(jnp.float32) + mixed1_mirror.astype(jnp.float32))).astype(
        jnp.bfloat16
    )
    return jnp.transpose(pair, (2, 0, 1))


def solution(mesh):
    placed = (P(("row", "col"), None), P(), P(), P(), P(), P())
    return jax.shard_map(
        local, mesh=mesh, in_specs=placed, out_specs=P(None, "row", "col"), check_vma=False
    )
```

```python
import jax
import jax.numpy as jnp
from jax import lax
from jax.experimental import pallas as pl
from jax.experimental.pallas import tpu as pltpu
from jax.sharding import PartitionSpec as P

MAXDIL = 4
REACH = 2 * MAXDIL


def gather_projections(proj):
    axes = ("row", "col")
    count = lax.axis_size("row") * lax.axis_size("col")
    flat = proj.reshape(2, -1)
    copies = jnp.broadcast_to(flat[None], (count,) + flat.shape)
    return lax.all_to_all(copies, axes, 0, 0, tiled=True).reshape(-1, proj.shape[1])


def inside(places, bins_total):
    return ((places >= 0) & (places < bins_total)).astype(jnp.float32)


CHUNK = 8


def row_group_kernel(dilation_ref, shifted_ref, weight_ref, out_ref):
    first = pl.program_id(0) * CHUNK + MAXDIL
    dilation = dilation_ref[0]
    cols, width = shifted_ref.shape[1], shifted_ref.shape[2]
    summed = None
    for outer in range(3):
        cells = shifted_ref[pl.ds(first + (outer - 1) * dilation, CHUNK), :, :]
        part = jnp.dot(
            cells.reshape(CHUNK * cols, width), weight_ref[outer], preferred_element_type=jnp.float32
        )
        summed = part if summed is None else summed + part
    out_ref[...] = summed.reshape(out_ref.shape)


def tap_groups(padded, weights, dilation):
    out_channels = weights.shape[1]
    in_channels = weights.shape[2]
    row_ext = padded.shape[0]
    row_count = row_ext - 2 * MAXDIL
    col_count = padded.shape[1] - 2 * MAXDIL
    zero_index = jnp.zeros((), jnp.int32)
    shifted = jnp.concatenate(
        [
            lax.dynamic_slice(
                padded,
                (zero_index, MAXDIL + (inner - 1) * dilation, zero_index),
                (row_ext, col_count, in_channels),
            )
            for inner in range(3)
        ],
        axis=2,
    )
    group_weight = jnp.transpose(weights, (0, 2, 1)).reshape(3, 3 * in_channels, out_channels)
    width = 3 * in_channels
    return pl.pallas_call(
        row_group_kernel,
        out_shape=jax.ShapeDtypeStruct((row_count, col_count, out_channels), jnp.float32),
        grid_spec=pltpu.PrefetchScalarGridSpec(
            num_scalar_prefetch=1,
            grid=(row_count // CHUNK,),
            in_specs=[
                pl.BlockSpec((row_ext, col_count, width), lambda g, d: (0, 0, 0)),
                pl.BlockSpec((3, width, out_channels), lambda g, d: (0, 0, 0)),
            ],
            out_specs=pl.BlockSpec((CHUNK, col_count, out_channels), lambda g, d: (g, 0, 0)),
        ),
    )(jnp.reshape(dilation, (1,)).astype(jnp.int32), shifted, group_weight)


def mirrored_taps(weights):
    return weights.reshape(3, 3, *weights.shape[1:]).swapaxes(0, 1).reshape(weights.shape)


def first_layer(every, taps, shift_bias, dilation, row_start, rows, col_start, cols):
    bins_total = every.shape[0]
    half = every.shape[1] // 2
    lower = jnp.arange(every.shape[1]) < half
    active = jnp.pad(jax.nn.relu(every), ((REACH, REACH), (0, 0)))
    padded = jnp.pad(every, ((MAXDIL, MAXDIL), (0, 0)))

    def tables(start, count):
        window = lax.dynamic_slice_in_dim(active, start, count + 2 * MAXDIL, 0)
        row_part = jnp.einsum(
            "nk,tok->tno", window[:, :half], taps[:, :, :half], preferred_element_type=jnp.float32
        )
        col_part = jnp.einsum(
            "nk,tok->tno", window[:, half:], taps[:, :, half:], preferred_element_type=jnp.float32
        )
        by_col, by_row = [], []
        for outer in range(3):
            along_rows = None
            along_cols = None
            for inner in range(3):
                piece_r = lax.dynamic_slice_in_dim(
                    row_part[3 * inner + outer], MAXDIL + (inner - 1) * dilation, count, 0
                )
                piece_c = lax.dynamic_slice_in_dim(
                    col_part[3 * outer + inner], MAXDIL + (inner - 1) * dilation, count, 0
                )
                along_rows = piece_r if along_rows is None else along_rows + piece_r
                along_cols = piece_c if along_cols is None else along_cols + piece_c
            by_col.append(along_rows)
            by_row.append(along_cols)
        own = lax.dynamic_slice_in_dim(padded, start, count, 0)
        own_row = jnp.where(lower, own, 0.0) + shift_bias[None, :]
        own_col = jnp.where(lower, 0.0, own)
        row_tables = [
            own_row + by_col[1] + by_col[2],
            own_row + by_col[0] + by_col[1] + by_col[2],
            own_row + by_col[0] + by_col[1],
        ]
        col_tables = [
            own_col + by_row[1] + by_row[2],
            own_col + by_row[0] + by_row[1] + by_row[2],
            own_col + by_row[0] + by_row[1],
        ]
        return row_tables, col_tables

    row_places = row_start - MAXDIL + jnp.arange(rows)
    col_places = col_start - MAXDIL + jnp.arange(cols)
    rows_row_tables, rows_col_tables = tables(row_start, rows)
    cols_row_tables, cols_col_tables = tables(col_start, cols)

    def pick(tables_here, places, axis):
        low, mid, high = tables_here
        shape = [1, 1, 1]
        shape[axis] = -1
        near_low = (places < dilation).reshape(shape)
        near_high = (places >= bins_total - dilation).reshape(shape)
        if axis == 1:
            low, mid, high = low[:, None, :], mid[:, None, :], high[:, None, :]
        else:
            low, mid, high = low[None, :, :], mid[None, :, :], high[None, :, :]
        return jnp.where(near_low, low, jnp.where(near_high, high, mid))

    mixed = (
        pick(rows_row_tables, col_places, 1) + pick(cols_col_tables, row_places, 0)
    ).astype(jnp.bfloat16)
    mixed_mirror = (
        pick(cols_row_tables, row_places, 0) + pick(rows_col_tables, col_places, 1)
    ).astype(jnp.bfloat16)
    return mixed, mixed_mirror, row_places, col_places


def local(features, row_weight, col_weight, conv_weight, conv_bias, dilations):
    both = jnp.concatenate([row_weight, col_weight], axis=1)
    proj = jnp.dot(features, both, preferred_element_type=jnp.float32).astype(jnp.bfloat16)
    every = gather_projections(proj)
    bins_total = every.shape[0]
    row_size = bins_total // lax.axis_size("row")
    col_size = bins_total // lax.axis_size("col")
    row_start = lax.axis_index("row") * row_size
    col_start = lax.axis_index("col") * col_size
    rows1 = row_size + 2 * MAXDIL
    cols1 = col_size + 2 * MAXDIL

    mixed0, mixed0_mirror, row_places, col_places = first_layer(
        every, conv_weight[0], conv_bias[0], dilations[0], row_start, rows1, col_start, cols1
    )
    map1 = (0.5 * (mixed0.astype(jnp.float32) + mixed0_mirror.astype(jnp.float32))).astype(
        jnp.bfloat16
    )

    mask1 = (
        inside(row_places, bins_total)[:, None, None] * inside(col_places, bins_total)[None, :, None]
    ).astype(jnp.bfloat16)
    taps1 = jnp.concatenate([conv_weight[1], mirrored_taps(conv_weight[1])], axis=1)
    conv1 = tap_groups(jax.nn.relu(map1) * mask1, taps1, dilations[1])
    channels = conv_weight.shape[2]
    core = (slice(MAXDIL, MAXDIL + row_size), slice(MAXDIL, MAXDIL + col_size), slice(None))
    base1 = map1[core].astype(jnp.float32) + conv_bias[1][None, None, :]
    mixed1 = (base1 + conv1[:, :, :channels]).astype(jnp.bfloat16)
    mixed1_mirror = (base1 + conv1[:, :, channels:]).astype(jnp.bfloat16)
    pair = (0.5 * (mixed1.astype(jnp.float32) + mixed1_mirror.astype(jnp.float32))).astype(
        jnp.bfloat16
    )
    return jnp.transpose(pair, (2, 0, 1))


def solution(mesh):
    placed = (P(("row", "col"), None), P(), P(), P(), P(), P())
    return jax.shard_map(
        local, mesh=mesh, in_specs=placed, out_specs=P(None, "row", "col"), check_vma=False
    )
```

```python
import jax
import jax.numpy as jnp
from jax import lax
from jax.sharding import PartitionSpec as P

MAXDIL = 4
REACH = 2 * MAXDIL


def gather_projections(proj):
    axes = ("row", "col")
    count = lax.axis_size("row") * lax.axis_size("col")
    flat = proj.reshape(2, -1)
    copies = jnp.broadcast_to(flat[None], (count,) + flat.shape)
    return lax.all_to_all(copies, axes, 0, 0, tiled=True).reshape(-1, proj.shape[1])


def inside(places, bins_total):
    return ((places >= 0) & (places < bins_total)).astype(jnp.float32)


def tap_groups(padded, weights, dilation):
    out_channels = weights.shape[1]
    in_channels = weights.shape[2]
    row_count = padded.shape[0] - 2 * MAXDIL
    col_count = padded.shape[1] - 2 * MAXDIL
    zero_index = jnp.zeros((), jnp.int32)
    pieces = []
    for tap in range(9):
        row_index = MAXDIL + (tap // 3 - 1) * dilation
        col_index = MAXDIL + (tap % 3 - 1) * dilation
        piece = lax.dynamic_slice(
            padded, (row_index, col_index, zero_index), (row_count, col_count, in_channels)
        )
        pieces.append(piece.reshape(row_count * col_count, in_channels))
    stacked = jnp.concatenate(pieces, axis=1)
    flat_weight = jnp.transpose(weights, (0, 2, 1)).reshape(9 * in_channels, out_channels)
    summed = jnp.dot(stacked, flat_weight, preferred_element_type=jnp.float32)
    return summed.reshape(row_count, col_count, out_channels)


def mirrored_taps(weights):
    return weights.reshape(3, 3, *weights.shape[1:]).swapaxes(0, 1).reshape(weights.shape)


def first_layer(every, taps, shift_bias, dilation, row_start, rows, col_start, cols):
    bins_total = every.shape[0]
    half = every.shape[1] // 2
    lower = jnp.arange(every.shape[1]) < half
    active = jnp.pad(jax.nn.relu(every), ((REACH, REACH), (0, 0)))
    padded = jnp.pad(every, ((MAXDIL, MAXDIL), (0, 0)))

    def tables(start, count):
        window = lax.dynamic_slice_in_dim(active, start, count + 2 * MAXDIL, 0)
        row_part = jnp.einsum(
            "nk,tok->tno", window[:, :half], taps[:, :, :half], preferred_element_type=jnp.float32
        )
        col_part = jnp.einsum(
            "nk,tok->tno", window[:, half:], taps[:, :, half:], preferred_element_type=jnp.float32
        )
        by_col, by_row = [], []
        for outer in range(3):
            along_rows = None
            along_cols = None
            for inner in range(3):
                piece_r = lax.dynamic_slice_in_dim(
                    row_part[3 * inner + outer], MAXDIL + (inner - 1) * dilation, count, 0
                )
                piece_c = lax.dynamic_slice_in_dim(
                    col_part[3 * outer + inner], MAXDIL + (inner - 1) * dilation, count, 0
                )
                along_rows = piece_r if along_rows is None else along_rows + piece_r
                along_cols = piece_c if along_cols is None else along_cols + piece_c
            by_col.append(along_rows)
            by_row.append(along_cols)
        own = lax.dynamic_slice_in_dim(padded, start, count, 0)
        own_row = jnp.where(lower, own, 0.0) + shift_bias[None, :]
        own_col = jnp.where(lower, 0.0, own)
        row_tables = [
            own_row + by_col[1] + by_col[2],
            own_row + by_col[0] + by_col[1] + by_col[2],
            own_row + by_col[0] + by_col[1],
        ]
        col_tables = [
            own_col + by_row[1] + by_row[2],
            own_col + by_row[0] + by_row[1] + by_row[2],
            own_col + by_row[0] + by_row[1],
        ]
        return row_tables, col_tables

    row_places = row_start - MAXDIL + jnp.arange(rows)
    col_places = col_start - MAXDIL + jnp.arange(cols)
    rows_row_tables, rows_col_tables = tables(row_start, rows)
    cols_row_tables, cols_col_tables = tables(col_start, cols)

    def pick(tables_here, places, axis):
        low, mid, high = tables_here
        shape = [1, 1, 1]
        shape[axis] = -1
        near_low = (places < dilation).reshape(shape)
        near_high = (places >= bins_total - dilation).reshape(shape)
        if axis == 1:
            low, mid, high = low[:, None, :], mid[:, None, :], high[:, None, :]
        else:
            low, mid, high = low[None, :, :], mid[None, :, :], high[None, :, :]
        return jnp.where(near_low, low, jnp.where(near_high, high, mid))

    mixed = (
        pick(rows_row_tables, col_places, 1) + pick(cols_col_tables, row_places, 0)
    ).astype(jnp.bfloat16)
    mixed_mirror = (
        pick(cols_row_tables, row_places, 0) + pick(rows_col_tables, col_places, 1)
    ).astype(jnp.bfloat16)
    return mixed, mixed_mirror, row_places, col_places


def local(features, row_weight, col_weight, conv_weight, conv_bias, dilations):
    both = jnp.concatenate([row_weight, col_weight], axis=1)
    proj = jnp.dot(features, both, preferred_element_type=jnp.float32).astype(jnp.bfloat16)
    every = gather_projections(proj)
    bins_total = every.shape[0]
    row_size = bins_total // lax.axis_size("row")
    col_size = bins_total // lax.axis_size("col")
    row_start = lax.axis_index("row") * row_size
    col_start = lax.axis_index("col") * col_size
    rows1 = row_size + 2 * MAXDIL
    cols1 = col_size + 2 * MAXDIL

    mixed0, mixed0_mirror, row_places, col_places = first_layer(
        every, conv_weight[0], conv_bias[0], dilations[0], row_start, rows1, col_start, cols1
    )
    map1 = (0.5 * (mixed0.astype(jnp.float32) + mixed0_mirror.astype(jnp.float32))).astype(
        jnp.bfloat16
    )

    mask1 = (
        inside(row_places, bins_total)[:, None, None] * inside(col_places, bins_total)[None, :, None]
    ).astype(jnp.bfloat16)
    taps1 = jnp.concatenate([conv_weight[1], mirrored_taps(conv_weight[1])], axis=1)
    conv1 = tap_groups(jax.nn.relu(map1) * mask1, taps1, dilations[1])
    channels = conv_weight.shape[2]
    core = (slice(MAXDIL, MAXDIL + row_size), slice(MAXDIL, MAXDIL + col_size), slice(None))
    base1 = map1[core].astype(jnp.float32) + conv_bias[1][None, None, :]
    mixed1 = (base1 + conv1[:, :, :channels]).astype(jnp.bfloat16)
    mixed1_mirror = (base1 + conv1[:, :, channels:]).astype(jnp.bfloat16)
    pair = (0.5 * (mixed1.astype(jnp.float32) + mixed1_mirror.astype(jnp.float32))).astype(
        jnp.bfloat16
    )
    flat = pair.reshape(row_size * col_size, channels)
    turned = jnp.einsum(
        "ck,nk->cn", jnp.eye(channels, dtype=pair.dtype), flat, preferred_element_type=jnp.float32
    )
    return turned.astype(jnp.bfloat16).reshape(channels, row_size, col_size)


def solution(mesh):
    placed = (P(("row", "col"), None), P(), P(), P(), P(), P())
    return jax.shard_map(
        local, mesh=mesh, in_specs=placed, out_specs=P(None, "row", "col"), check_vma=False
    )
```

```python
import jax
import jax.numpy as jnp
from jax import lax
from jax.sharding import PartitionSpec as P

MAXDIL = 4
REACH = 2 * MAXDIL


def gather_projections(proj):
    axes = ("row", "col")
    count = lax.axis_size("row") * lax.axis_size("col")
    flat = proj.reshape(2, -1)
    copies = jnp.broadcast_to(flat[None], (count,) + flat.shape)
    return lax.all_to_all(copies, axes, 0, 0, tiled=True).reshape(-1, proj.shape[1])


def inside(places, bins_total):
    return ((places >= 0) & (places < bins_total)).astype(jnp.float32)


def tap_groups(padded, weights, dilation):
    out_channels = weights.shape[1]
    in_channels = weights.shape[2]
    row_count = padded.shape[0] - 2 * MAXDIL
    col_count = padded.shape[1] - 2 * MAXDIL
    zero_index = jnp.zeros((), jnp.int32)
    pieces = []
    for tap in range(9):
        row_index = MAXDIL + (tap // 3 - 1) * dilation
        col_index = MAXDIL + (tap % 3 - 1) * dilation
        piece = lax.dynamic_slice(
            padded,
            (row_index, col_index, zero_index + (tap % 2) * in_channels),
            (row_count, col_count, in_channels),
        )
        pieces.append(piece.reshape(row_count * col_count, in_channels))
    stacked = jnp.concatenate(pieces, axis=1)
    flat_weight = jnp.transpose(weights, (0, 2, 1)).reshape(9 * in_channels, out_channels)
    summed = jnp.dot(stacked, flat_weight, preferred_element_type=jnp.float32)
    return summed.reshape(row_count, col_count, out_channels)


def mirrored_taps(weights):
    return weights.reshape(3, 3, *weights.shape[1:]).swapaxes(0, 1).reshape(weights.shape)


def first_layer(every, taps, shift_bias, dilation, row_start, rows, col_start, cols):
    bins_total = every.shape[0]
    channels = every.shape[1]
    half = channels // 2
    lower = (jnp.arange(2 * channels) % channels) < half
    taps = jnp.concatenate([taps, taps], axis=1)
    shift_bias = jnp.concatenate([shift_bias, shift_bias])
    active = jnp.pad(jax.nn.relu(every), ((REACH, REACH), (0, 0)))
    padded = jnp.pad(every, ((MAXDIL, MAXDIL), (0, 0)))

    def tables(start, count):
        window = lax.dynamic_slice_in_dim(active, start, count + 2 * MAXDIL, 0)
        row_part = jnp.einsum(
            "nk,tok->tno", window[:, :half], taps[:, :, :half], preferred_element_type=jnp.float32
        )
        col_part = jnp.einsum(
            "nk,tok->tno", window[:, half:], taps[:, :, half:], preferred_element_type=jnp.float32
        )
        by_col, by_row = [], []
        for outer in range(3):
            along_rows = None
            along_cols = None
            for inner in range(3):
                piece_r = lax.dynamic_slice_in_dim(
                    row_part[3 * inner + outer], MAXDIL + (inner - 1) * dilation, count, 0
                )
                piece_c = lax.dynamic_slice_in_dim(
                    col_part[3 * outer + inner], MAXDIL + (inner - 1) * dilation, count, 0
                )
                along_rows = piece_r if along_rows is None else along_rows + piece_r
                along_cols = piece_c if along_cols is None else along_cols + piece_c
            by_col.append(along_rows)
            by_row.append(along_cols)
        own = lax.dynamic_slice_in_dim(padded, start, count, 0)
        own = jnp.concatenate([own, own], axis=1)
        own_row = jnp.where(lower, own, 0.0) + shift_bias[None, :]
        own_col = jnp.where(lower, 0.0, own)
        row_tables = [
            own_row + by_col[1] + by_col[2],
            own_row + by_col[0] + by_col[1] + by_col[2],
            own_row + by_col[0] + by_col[1],
        ]
        col_tables = [
            own_col + by_row[1] + by_row[2],
            own_col + by_row[0] + by_row[1] + by_row[2],
            own_col + by_row[0] + by_row[1],
        ]
        return row_tables, col_tables

    row_places = row_start - MAXDIL + jnp.arange(rows)
    col_places = col_start - MAXDIL + jnp.arange(cols)
    rows_row_tables, rows_col_tables = tables(row_start, rows)
    cols_row_tables, cols_col_tables = tables(col_start, cols)

    def pick(tables_here, places, axis):
        low, mid, high = tables_here
        shape = [1, 1, 1]
        shape[axis] = -1
        near_low = (places < dilation).reshape(shape)
        near_high = (places >= bins_total - dilation).reshape(shape)
        if axis == 1:
            low, mid, high = low[:, None, :], mid[:, None, :], high[:, None, :]
        else:
            low, mid, high = low[None, :, :], mid[None, :, :], high[None, :, :]
        return jnp.where(near_low, low, jnp.where(near_high, high, mid))

    mixed = (
        pick(rows_row_tables, col_places, 1) + pick(cols_col_tables, row_places, 0)
    ).astype(jnp.bfloat16)
    mixed_mirror = (
        pick(cols_row_tables, row_places, 0) + pick(rows_col_tables, col_places, 1)
    ).astype(jnp.bfloat16)
    return mixed, mixed_mirror, row_places, col_places


def local(features, row_weight, col_weight, conv_weight, conv_bias, dilations):
    both = jnp.concatenate([row_weight, col_weight], axis=1)
    proj = jnp.dot(features, both, preferred_element_type=jnp.float32).astype(jnp.bfloat16)
    every = gather_projections(proj)
    bins_total = every.shape[0]
    row_size = bins_total // lax.axis_size("row")
    col_size = bins_total // lax.axis_size("col")
    row_start = lax.axis_index("row") * row_size
    col_start = lax.axis_index("col") * col_size
    rows1 = row_size + 2 * MAXDIL
    cols1 = col_size + 2 * MAXDIL

    mixed0, mixed0_mirror, row_places, col_places = first_layer(
        every, conv_weight[0], conv_bias[0], dilations[0], row_start, rows1, col_start, cols1
    )
    map1 = (0.5 * (mixed0.astype(jnp.float32) + mixed0_mirror.astype(jnp.float32))).astype(
        jnp.bfloat16
    )

    mask1 = (
        inside(row_places, bins_total)[:, None, None] * inside(col_places, bins_total)[None, :, None]
    ).astype(jnp.bfloat16)
    taps1 = jnp.concatenate([conv_weight[1], mirrored_taps(conv_weight[1])], axis=1)
    conv1 = tap_groups(jax.nn.relu(map1) * mask1, taps1, dilations[1])
    channels = conv_weight.shape[2]
    core = (slice(MAXDIL, MAXDIL + row_size), slice(MAXDIL, MAXDIL + col_size), slice(None))
    base1 = map1[core][:, :, :channels].astype(jnp.float32) + conv_bias[1][None, None, :]
    mixed1 = (base1 + conv1[:, :, :channels]).astype(jnp.bfloat16)
    mixed1_mirror = (base1 + conv1[:, :, channels:]).astype(jnp.bfloat16)
    pair = (0.5 * (mixed1.astype(jnp.float32) + mixed1_mirror.astype(jnp.float32))).astype(
        jnp.bfloat16
    )
    flat = pair.reshape(row_size * col_size, channels)
    turned = jnp.einsum(
        "ck,nk->cn", jnp.eye(channels, dtype=pair.dtype), flat, preferred_element_type=jnp.float32
    )
    return turned.astype(jnp.bfloat16).reshape(channels, row_size, col_size)


def solution(mesh):
    placed = (P(("row", "col"), None), P(), P(), P(), P(), P())
    return jax.shard_map(
        local, mesh=mesh, in_specs=placed, out_specs=P(None, "row", "col"), check_vma=False
    )
```

```python
import jax
import jax.numpy as jnp
from jax import lax
from jax.sharding import PartitionSpec as P

MAXDIL = 4
REACH = 2 * MAXDIL


def gather_projections(proj):
    axes = ("row", "col")
    count = lax.axis_size("row") * lax.axis_size("col")
    flat = proj.reshape(2, -1)
    copies = jnp.broadcast_to(flat[None], (count,) + flat.shape)
    return lax.all_to_all(copies, axes, 0, 0, tiled=True).reshape(-1, proj.shape[1])


def inside(places, bins_total):
    return ((places >= 0) & (places < bins_total)).astype(jnp.float32)


def tap_groups(padded, weights, dilation):
    out_channels = weights.shape[1]
    in_channels = weights.shape[2]
    row_count = padded.shape[0] - 2 * MAXDIL
    col_count = padded.shape[1] - 2 * MAXDIL
    zero_index = jnp.zeros((), jnp.int32)
    pieces = []
    for tap in range(9):
        row_index = MAXDIL + (tap // 3 - 1) * dilation
        col_index = MAXDIL + (tap % 3 - 1) * dilation
        piece = lax.dynamic_slice(
            padded, (row_index, col_index, zero_index), (row_count, col_count, in_channels)
        )
        pieces.append(piece.reshape(row_count * col_count, in_channels).astype(jnp.bfloat16))
    stacked = jnp.concatenate(pieces, axis=1)
    flat_weight = jnp.transpose(weights, (0, 2, 1)).reshape(9 * in_channels, out_channels)
    summed = jnp.dot(stacked, flat_weight, preferred_element_type=jnp.float32)
    return summed.reshape(row_count, col_count, out_channels)


def mirrored_taps(weights):
    return weights.reshape(3, 3, *weights.shape[1:]).swapaxes(0, 1).reshape(weights.shape)


def first_layer(every, taps, shift_bias, dilation, row_start, rows, col_start, cols):
    bins_total = every.shape[0]
    half = every.shape[1] // 2
    lower = jnp.arange(every.shape[1]) < half
    active = jnp.pad(jax.nn.relu(every), ((REACH, REACH), (0, 0)))
    padded = jnp.pad(every, ((MAXDIL, MAXDIL), (0, 0)))

    def tables(start, count):
        window = lax.dynamic_slice_in_dim(active, start, count + 2 * MAXDIL, 0)
        row_part = jnp.einsum(
            "nk,tok->tno", window[:, :half], taps[:, :, :half], preferred_element_type=jnp.float32
        )
        col_part = jnp.einsum(
            "nk,tok->tno", window[:, half:], taps[:, :, half:], preferred_element_type=jnp.float32
        )
        by_col, by_row = [], []
        for outer in range(3):
            along_rows = None
            along_cols = None
            for inner in range(3):
                piece_r = lax.dynamic_slice_in_dim(
                    row_part[3 * inner + outer], MAXDIL + (inner - 1) * dilation, count, 0
                )
                piece_c = lax.dynamic_slice_in_dim(
                    col_part[3 * outer + inner], MAXDIL + (inner - 1) * dilation, count, 0
                )
                along_rows = piece_r if along_rows is None else along_rows + piece_r
                along_cols = piece_c if along_cols is None else along_cols + piece_c
            by_col.append(along_rows)
            by_row.append(along_cols)
        own = lax.dynamic_slice_in_dim(padded, start, count, 0)
        own_row = jnp.where(lower, own, 0.0) + shift_bias[None, :]
        own_col = jnp.where(lower, 0.0, own)
        row_tables = [
            own_row + by_col[1] + by_col[2],
            own_row + by_col[0] + by_col[1] + by_col[2],
            own_row + by_col[0] + by_col[1],
        ]
        col_tables = [
            own_col + by_row[1] + by_row[2],
            own_col + by_row[0] + by_row[1] + by_row[2],
            own_col + by_row[0] + by_row[1],
        ]
        return row_tables, col_tables

    row_places = row_start - MAXDIL + jnp.arange(rows)
    col_places = col_start - MAXDIL + jnp.arange(cols)
    rows_row_tables, rows_col_tables = tables(row_start, rows)
    cols_row_tables, cols_col_tables = tables(col_start, cols)

    def pick(tables_here, places, axis):
        low, mid, high = tables_here
        shape = [1, 1, 1]
        shape[axis] = -1
        near_low = (places < dilation).reshape(shape)
        near_high = (places >= bins_total - dilation).reshape(shape)
        if axis == 1:
            low, mid, high = low[:, None, :], mid[:, None, :], high[:, None, :]
        else:
            low, mid, high = low[None, :, :], mid[None, :, :], high[None, :, :]
        return jnp.where(near_low, low, jnp.where(near_high, high, mid))

    mixed = (
        pick(rows_row_tables, col_places, 1) + pick(cols_col_tables, row_places, 0)
    ).astype(jnp.bfloat16)
    mixed_mirror = (
        pick(cols_row_tables, row_places, 0) + pick(rows_col_tables, col_places, 1)
    ).astype(jnp.bfloat16)
    return mixed, mixed_mirror, row_places, col_places


def local(features, row_weight, col_weight, conv_weight, conv_bias, dilations):
    both = jnp.concatenate([row_weight, col_weight], axis=1)
    proj = jnp.dot(features, both, preferred_element_type=jnp.float32).astype(jnp.bfloat16)
    every = gather_projections(proj)
    bins_total = every.shape[0]
    row_size = bins_total // lax.axis_size("row")
    col_size = bins_total // lax.axis_size("col")
    row_start = lax.axis_index("row") * row_size
    col_start = lax.axis_index("col") * col_size
    rows1 = row_size + 2 * MAXDIL
    cols1 = col_size + 2 * MAXDIL

    mixed0, mixed0_mirror, row_places, col_places = first_layer(
        every, conv_weight[0], conv_bias[0], dilations[0], row_start, rows1, col_start, cols1
    )
    map1 = (0.5 * (mixed0.astype(jnp.float32) + mixed0_mirror.astype(jnp.float32))).astype(
        jnp.bfloat16
    )

    mask1 = (
        inside(row_places, bins_total)[:, None, None] * inside(col_places, bins_total)[None, :, None]
    ).astype(jnp.bfloat16)
    taps1 = jnp.concatenate([conv_weight[1], mirrored_taps(conv_weight[1])], axis=1)
    active1 = jax.nn.relu(map1).astype(jnp.float32) * mask1.astype(jnp.float32)
    conv1 = tap_groups(active1, taps1, dilations[1])
    channels = conv_weight.shape[2]
    core = (slice(MAXDIL, MAXDIL + row_size), slice(MAXDIL, MAXDIL + col_size), slice(None))
    base1 = map1[core].astype(jnp.float32) + conv_bias[1][None, None, :]
    mixed1 = (base1 + conv1[:, :, :channels]).astype(jnp.bfloat16)
    mixed1_mirror = (base1 + conv1[:, :, channels:]).astype(jnp.bfloat16)
    pair = (0.5 * (mixed1.astype(jnp.float32) + mixed1_mirror.astype(jnp.float32))).astype(
        jnp.bfloat16
    )
    flat = pair.reshape(row_size * col_size, channels)
    turned = jnp.einsum(
        "ck,nk->cn", jnp.eye(channels, dtype=pair.dtype), flat, preferred_element_type=jnp.float32
    )
    return turned.astype(jnp.bfloat16).reshape(channels, row_size, col_size)


def solution(mesh):
    placed = (P(("row", "col"), None), P(), P(), P(), P(), P())
    return jax.shard_map(
        local, mesh=mesh, in_specs=placed, out_specs=P(None, "row", "col"), check_vma=False
    )
```

```python
import jax
import jax.numpy as jnp
from jax import lax
from jax.sharding import PartitionSpec as P

MAXDIL = 4
REACH = 2 * MAXDIL


def gather_projections(proj):
    axes = ("row", "col")
    count = lax.axis_size("row") * lax.axis_size("col")
    flat = proj.reshape(2, -1)
    copies = jnp.broadcast_to(flat[None], (count,) + flat.shape)
    return lax.all_to_all(copies, axes, 0, 0, tiled=True).reshape(-1, proj.shape[1])


def inside(places, bins_total):
    return ((places >= 0) & (places < bins_total)).astype(jnp.float32)


def tap_groups(padded, weights, dilation):
    out_channels = weights.shape[1]
    in_channels = weights.shape[2]
    row_count = padded.shape[0] - 2 * MAXDIL
    col_count = padded.shape[1] - 2 * MAXDIL
    zero_index = jnp.zeros((), jnp.int32)
    pieces = []
    for tap in range(9):
        row_index = MAXDIL + (tap // 3 - 1) * dilation
        col_index = MAXDIL + (tap % 3 - 1) * dilation
        piece = lax.dynamic_slice(
            padded, (row_index, col_index, zero_index), (row_count, col_count, in_channels)
        )
        pieces.append(piece.reshape(row_count * col_count, in_channels))
    stacked = jnp.concatenate(pieces, axis=1)
    flat_weight = jnp.transpose(weights, (0, 2, 1)).reshape(9 * in_channels, out_channels)
    summed = jnp.dot(stacked, flat_weight, preferred_element_type=jnp.float32)
    return summed.reshape(row_count, col_count, out_channels)


def mirrored_taps(weights):
    return weights.reshape(3, 3, *weights.shape[1:]).swapaxes(0, 1).reshape(weights.shape)


def first_layer(every, taps, shift_bias, dilation, row_start, rows, col_start, cols):
    bins_total = every.shape[0]
    half = every.shape[1] // 2
    lower = jnp.arange(every.shape[1]) < half
    active = jnp.pad(jax.nn.relu(every), ((REACH, REACH), (0, 0)))
    padded = jnp.pad(every, ((MAXDIL, MAXDIL), (0, 0)))

    grid = taps.reshape(3, 3, *taps.shape[1:])
    out_ch = taps.shape[1]
    by_shift_row = jnp.transpose(grid[..., :half], (0, 3, 1, 2)).reshape(3, half, 3 * out_ch)
    by_shift_col = jnp.transpose(grid[..., half:], (1, 3, 0, 2)).reshape(3, half, 3 * out_ch)
    nothing = jnp.zeros_like(by_shift_row)
    weight = jnp.concatenate(
        [
            jnp.concatenate([by_shift_row, nothing], axis=2),
            jnp.concatenate([nothing, by_shift_col], axis=2),
        ],
        axis=1,
    ).reshape(3 * 2 * half, 6 * out_ch)

    def tables(start, count):
        window = lax.dynamic_slice_in_dim(active, start, count + 2 * MAXDIL, 0)
        shifted = jnp.concatenate(
            [
                lax.dynamic_slice_in_dim(window, MAXDIL + (step - 1) * dilation, count, 0)
                for step in range(3)
            ],
            axis=1,
        )
        parts = jnp.dot(shifted, weight, preferred_element_type=jnp.float32)
        by_col = [parts[:, out_ch * k : out_ch * (k + 1)] for k in range(3)]
        by_row = [parts[:, out_ch * (3 + k) : out_ch * (4 + k)] for k in range(3)]
        own = lax.dynamic_slice_in_dim(padded, start, count, 0)
        own_row = jnp.where(lower, own, 0.0) + shift_bias[None, :]
        own_col = jnp.where(lower, 0.0, own)
        row_tables = [
            own_row + by_col[1] + by_col[2],
            own_row + by_col[0] + by_col[1] + by_col[2],
            own_row + by_col[0] + by_col[1],
        ]
        col_tables = [
            own_col + by_row[1] + by_row[2],
            own_col + by_row[0] + by_row[1] + by_row[2],
            own_col + by_row[0] + by_row[1],
        ]
        return row_tables, col_tables

    row_places = row_start - MAXDIL + jnp.arange(rows)
    col_places = col_start - MAXDIL + jnp.arange(cols)
    rows_row_tables, rows_col_tables = tables(row_start, rows)
    cols_row_tables, cols_col_tables = tables(col_start, cols)

    def pick(tables_here, places, axis):
        low, mid, high = tables_here
        shape = [1, 1, 1]
        shape[axis] = -1
        near_low = (places < dilation).reshape(shape)
        near_high = (places >= bins_total - dilation).reshape(shape)
        if axis == 1:
            low, mid, high = low[:, None, :], mid[:, None, :], high[:, None, :]
        else:
            low, mid, high = low[None, :, :], mid[None, :, :], high[None, :, :]
        return jnp.where(near_low, low, jnp.where(near_high, high, mid))

    mixed = (
        pick(rows_row_tables, col_places, 1) + pick(cols_col_tables, row_places, 0)
    ).astype(jnp.bfloat16)
    mixed_mirror = (
        pick(cols_row_tables, row_places, 0) + pick(rows_col_tables, col_places, 1)
    ).astype(jnp.bfloat16)
    return mixed, mixed_mirror, row_places, col_places


def local(features, row_weight, col_weight, conv_weight, conv_bias, dilations):
    both = jnp.concatenate([row_weight, col_weight], axis=1)
    proj = jnp.dot(features, both, preferred_element_type=jnp.float32).astype(jnp.bfloat16)
    every = gather_projections(proj)
    bins_total = every.shape[0]
    row_size = bins_total // lax.axis_size("row")
    col_size = bins_total // lax.axis_size("col")
    row_start = lax.axis_index("row") * row_size
    col_start = lax.axis_index("col") * col_size
    rows1 = row_size + 2 * MAXDIL
    cols1 = col_size + 2 * MAXDIL

    mixed0, mixed0_mirror, row_places, col_places = first_layer(
        every, conv_weight[0], conv_bias[0], dilations[0], row_start, rows1, col_start, cols1
    )
    map1 = (0.5 * (mixed0.astype(jnp.float32) + mixed0_mirror.astype(jnp.float32))).astype(
        jnp.bfloat16
    )

    mask1 = (
        inside(row_places, bins_total)[:, None, None] * inside(col_places, bins_total)[None, :, None]
    ).astype(jnp.bfloat16)
    taps1 = jnp.concatenate([conv_weight[1], mirrored_taps(conv_weight[1])], axis=1)
    conv1 = tap_groups(jax.nn.relu(map1) * mask1, taps1, dilations[1])
    channels = conv_weight.shape[2]
    core = (slice(MAXDIL, MAXDIL + row_size), slice(MAXDIL, MAXDIL + col_size), slice(None))
    base1 = map1[core].astype(jnp.float32) + conv_bias[1][None, None, :]
    mixed1 = (base1 + conv1[:, :, :channels]).astype(jnp.bfloat16)
    mixed1_mirror = (base1 + conv1[:, :, channels:]).astype(jnp.bfloat16)
    pair = (0.5 * (mixed1.astype(jnp.float32) + mixed1_mirror.astype(jnp.float32))).astype(
        jnp.bfloat16
    )
    flat = pair.reshape(row_size * col_size, channels)
    turned = jnp.einsum(
        "ck,nk->cn", jnp.eye(channels, dtype=pair.dtype), flat, preferred_element_type=jnp.float32
    )
    return turned.astype(jnp.bfloat16).reshape(channels, row_size, col_size)


def solution(mesh):
    placed = (P(("row", "col"), None), P(), P(), P(), P(), P())
    return jax.shard_map(
        local, mesh=mesh, in_specs=placed, out_specs=P(None, "row", "col"), check_vma=False
    )
```

```python
import jax
import jax.numpy as jnp
from jax import lax
from jax.sharding import PartitionSpec as P

MAXDIL = 4
REACH = 2 * MAXDIL


def gather_projections(proj):
    axes = ("row", "col")
    count = lax.axis_size("row") * lax.axis_size("col")
    flat = proj.reshape(2, -1)
    copies = jnp.broadcast_to(flat[None], (count,) + flat.shape)
    return lax.all_to_all(copies, axes, 0, 0, tiled=True).reshape(-1, proj.shape[1])


def inside(places, bins_total):
    return ((places >= 0) & (places < bins_total)).astype(jnp.float32)


def tap_groups(padded, weights, dilation):
    out_channels = weights.shape[1]
    in_channels = weights.shape[2]
    row_count = padded.shape[0] - 2 * MAXDIL
    col_count = padded.shape[1] - 2 * MAXDIL
    zero_index = jnp.zeros((), jnp.int32)
    pieces = []
    for tap in range(9):
        row_index = MAXDIL + (tap // 3 - 1) * dilation
        col_index = MAXDIL + (tap % 3 - 1) * dilation
        piece = lax.dynamic_slice(
            padded, (row_index, col_index, zero_index), (row_count, col_count, in_channels)
        )
        pieces.append(piece.reshape(row_count * col_count, in_channels))
    stacked = jnp.concatenate(pieces, axis=1)
    flat_weight = jnp.transpose(weights, (0, 2, 1)).reshape(9 * in_channels, out_channels)
    summed = jnp.dot(stacked, flat_weight, preferred_element_type=jnp.float32)
    return summed.reshape(row_count, col_count, out_channels)


def mirrored_taps(weights):
    return weights.reshape(3, 3, *weights.shape[1:]).swapaxes(0, 1).reshape(weights.shape)


def first_layer(every, taps, shift_bias, dilation, row_start, rows, col_start, cols):
    bins_total = every.shape[0]
    half = every.shape[1] // 2
    lower = jnp.arange(every.shape[1]) < half
    active = jnp.pad(jax.nn.relu(every), ((REACH, REACH), (0, 0)))
    padded = jnp.pad(every, ((MAXDIL, MAXDIL), (0, 0)))

    grid = taps.reshape(3, 3, *taps.shape[1:])
    out_ch = taps.shape[1]
    by_shift_row = jnp.transpose(grid[..., :half], (0, 3, 1, 2)).reshape(3, half, 3 * out_ch)
    by_shift_col = jnp.transpose(grid[..., half:], (1, 3, 0, 2)).reshape(3, half, 3 * out_ch)
    lane_group = 2 * out_ch
    by_shift_row, by_shift_col = (
        jnp.pad(w.reshape(3, half, 3, out_ch), ((0, 0), (0, 0), (0, 0), (0, lane_group - out_ch))).reshape(
            3, half, 3 * lane_group
        )
        for w in (by_shift_row, by_shift_col)
    )
    nothing = jnp.zeros_like(by_shift_row)
    weight = jnp.concatenate(
        [
            jnp.concatenate([by_shift_row, nothing], axis=2),
            jnp.concatenate([nothing, by_shift_col], axis=2),
        ],
        axis=1,
    ).reshape(3 * 2 * half, 6 * lane_group)

    def tables(start, count):
        window = lax.dynamic_slice_in_dim(active, start, count + 2 * MAXDIL, 0)
        shifted = jnp.concatenate(
            [
                lax.dynamic_slice_in_dim(window, MAXDIL + (step - 1) * dilation, count, 0)
                for step in range(3)
            ],
            axis=1,
        )
        parts = jnp.dot(shifted, weight, preferred_element_type=jnp.float32)
        by_col = [parts[:, lane_group * k : lane_group * k + out_ch] for k in range(3)]
        by_row = [parts[:, lane_group * (3 + k) : lane_group * (3 + k) + out_ch] for k in range(3)]
        own = lax.dynamic_slice_in_dim(padded, start, count, 0)
        own_row = jnp.where(lower, own, 0.0) + shift_bias[None, :]
        own_col = jnp.where(lower, 0.0, own)
        row_tables = [
            own_row + by_col[1] + by_col[2],
            own_row + by_col[0] + by_col[1] + by_col[2],
            own_row + by_col[0] + by_col[1],
        ]
        col_tables = [
            own_col + by_row[1] + by_row[2],
            own_col + by_row[0] + by_row[1] + by_row[2],
            own_col + by_row[0] + by_row[1],
        ]
        return row_tables, col_tables

    row_places = row_start - MAXDIL + jnp.arange(rows)
    col_places = col_start - MAXDIL + jnp.arange(cols)
    rows_row_tables, rows_col_tables = tables(row_start, rows)
    cols_row_tables, cols_col_tables = tables(col_start, cols)

    def pick(tables_here, places, axis):
        low, mid, high = tables_here
        shape = [1, 1, 1]
        shape[axis] = -1
        near_low = (places < dilation).reshape(shape)
        near_high = (places >= bins_total - dilation).reshape(shape)
        if axis == 1:
            low, mid, high = low[:, None, :], mid[:, None, :], high[:, None, :]
        else:
            low, mid, high = low[None, :, :], mid[None, :, :], high[None, :, :]
        return jnp.where(near_low, low, jnp.where(near_high, high, mid))

    mixed = (
        pick(rows_row_tables, col_places, 1) + pick(cols_col_tables, row_places, 0)
    ).astype(jnp.bfloat16)
    mixed_mirror = (
        pick(cols_row_tables, row_places, 0) + pick(rows_col_tables, col_places, 1)
    ).astype(jnp.bfloat16)
    return mixed, mixed_mirror, row_places, col_places


def local(features, row_weight, col_weight, conv_weight, conv_bias, dilations):
    both = jnp.concatenate([row_weight, col_weight], axis=1)
    proj = jnp.dot(features, both, preferred_element_type=jnp.float32).astype(jnp.bfloat16)
    every = gather_projections(proj)
    bins_total = every.shape[0]
    row_size = bins_total // lax.axis_size("row")
    col_size = bins_total // lax.axis_size("col")
    row_start = lax.axis_index("row") * row_size
    col_start = lax.axis_index("col") * col_size
    rows1 = row_size + 2 * MAXDIL
    cols1 = col_size + 2 * MAXDIL

    mixed0, mixed0_mirror, row_places, col_places = first_layer(
        every, conv_weight[0], conv_bias[0], dilations[0], row_start, rows1, col_start, cols1
    )
    map1 = (0.5 * (mixed0.astype(jnp.float32) + mixed0_mirror.astype(jnp.float32))).astype(
        jnp.bfloat16
    )

    mask1 = (
        inside(row_places, bins_total)[:, None, None] * inside(col_places, bins_total)[None, :, None]
    ).astype(jnp.bfloat16)
    taps1 = jnp.concatenate([conv_weight[1], mirrored_taps(conv_weight[1])], axis=1)
    conv1 = tap_groups(jax.nn.relu(map1) * mask1, taps1, dilations[1])
    channels = conv_weight.shape[2]
    core = (slice(MAXDIL, MAXDIL + row_size), slice(MAXDIL, MAXDIL + col_size), slice(None))
    base1 = map1[core].astype(jnp.float32) + conv_bias[1][None, None, :]
    mixed1 = (base1 + conv1[:, :, :channels]).astype(jnp.bfloat16)
    mixed1_mirror = (base1 + conv1[:, :, channels:]).astype(jnp.bfloat16)
    pair = (0.5 * (mixed1.astype(jnp.float32) + mixed1_mirror.astype(jnp.float32))).astype(
        jnp.bfloat16
    )
    flat = pair.reshape(row_size * col_size, channels)
    turned = jnp.einsum(
        "ck,nk->cn", jnp.eye(channels, dtype=pair.dtype), flat, preferred_element_type=jnp.float32
    )
    return turned.astype(jnp.bfloat16).reshape(channels, row_size, col_size)


def solution(mesh):
    placed = (P(("row", "col"), None), P(), P(), P(), P(), P())
    return jax.shard_map(
        local, mesh=mesh, in_specs=placed, out_specs=P(None, "row", "col"), check_vma=False
    )
```

```python
import jax
import jax.numpy as jnp
from jax import lax
from jax.sharding import PartitionSpec as P

MAXDIL = 4
REACH = 2 * MAXDIL


def gather_projections(proj):
    axes = ("row", "col")
    count = lax.axis_size("row") * lax.axis_size("col")
    flat = proj.reshape(2, -1)
    copies = jnp.broadcast_to(flat[None], (count,) + flat.shape)
    return lax.all_to_all(copies, axes, 0, 0, tiled=True).reshape(-1, proj.shape[1])


def inside(places, bins_total):
    return ((places >= 0) & (places < bins_total)).astype(jnp.float32)


def tap_groups(padded, weights, dilation):
    out_channels = weights.shape[1]
    in_channels = weights.shape[2]
    row_count = padded.shape[0] - 2 * MAXDIL
    col_count = padded.shape[1] - 2 * MAXDIL
    zero_index = jnp.zeros((), jnp.int32)
    pieces = []
    for tap in range(9):
        row_index = MAXDIL + (tap // 3 - 1) * dilation
        col_index = MAXDIL + (tap % 3 - 1) * dilation
        piece = lax.dynamic_slice(
            padded, (row_index, col_index, zero_index), (row_count, col_count, in_channels)
        )
        pieces.append(piece.reshape(row_count * col_count, in_channels))
    stacked = jnp.concatenate(pieces, axis=1)
    flat_weight = jnp.transpose(weights, (0, 2, 1)).reshape(9 * in_channels, out_channels)
    summed = jnp.dot(stacked, flat_weight, preferred_element_type=jnp.float32)
    return summed.reshape(row_count, col_count, out_channels)


def mirrored_taps(weights):
    return weights.reshape(3, 3, *weights.shape[1:]).swapaxes(0, 1).reshape(weights.shape)


def first_layer(every, taps, shift_bias, dilation, row_start, rows, col_start, cols):
    bins_total = every.shape[0]
    half = every.shape[1] // 2
    lower = jnp.arange(every.shape[1]) < half
    active = jnp.pad(jax.nn.relu(every), ((REACH, REACH), (0, 0)))
    padded = jnp.pad(every, ((MAXDIL, MAXDIL), (0, 0)))

    grid = taps.reshape(3, 3, *taps.shape[1:])
    out_ch = taps.shape[1]
    by_shift_row = jnp.transpose(grid[..., :half], (0, 3, 1, 2)).reshape(3, half, 3 * out_ch)
    by_shift_col = jnp.transpose(grid[..., half:], (1, 3, 0, 2)).reshape(3, half, 3 * out_ch)
    lane_group = 2 * out_ch
    by_shift_row, by_shift_col = (
        jnp.pad(w.reshape(3, half, 3, out_ch), ((0, 0), (0, 0), (0, 0), (0, lane_group - out_ch))).reshape(
            3, half, 3 * lane_group
        )
        for w in (by_shift_row, by_shift_col)
    )
    nothing = jnp.zeros_like(by_shift_row)
    weight = jnp.concatenate(
        [
            jnp.concatenate([by_shift_row, nothing], axis=2),
            jnp.concatenate([nothing, by_shift_col], axis=2),
        ],
        axis=1,
    ).reshape(3 * 2 * half, 6 * lane_group)

    def tables(start, count):
        window = lax.dynamic_slice_in_dim(active, start, count + 2 * MAXDIL, 0)
        shifted = jnp.concatenate(
            [
                lax.dynamic_slice_in_dim(window, MAXDIL + (step - 1) * dilation, count, 0)
                for step in range(3)
            ],
            axis=1,
        )
        parts = jnp.dot(shifted, weight, preferred_element_type=jnp.float32)
        by_col = [parts[:, lane_group * k : lane_group * k + out_ch] for k in range(3)]
        by_row = [parts[:, lane_group * (3 + k) : lane_group * (3 + k) + out_ch] for k in range(3)]
        own = lax.dynamic_slice_in_dim(padded, start, count, 0)
        own_row = jnp.where(lower, own, 0.0) + shift_bias[None, :]
        own_col = jnp.where(lower, 0.0, own)
        row_tables = [
            own_row + by_col[1] + by_col[2],
            own_row + by_col[0] + by_col[1] + by_col[2],
            own_row + by_col[0] + by_col[1],
        ]
        col_tables = [
            own_col + by_row[1] + by_row[2],
            own_col + by_row[0] + by_row[1] + by_row[2],
            own_col + by_row[0] + by_row[1],
        ]
        return row_tables, col_tables

    row_places = row_start - MAXDIL + jnp.arange(rows)
    col_places = col_start - MAXDIL + jnp.arange(cols)
    rows_row_tables, rows_col_tables = tables(row_start, rows)
    cols_row_tables, cols_col_tables = tables(col_start, cols)

    def pick(tables_here, places, axis):
        low, mid, high = tables_here
        shape = [1, 1, 1]
        shape[axis] = -1
        near_low = (places < dilation).reshape(shape)
        near_high = (places >= bins_total - dilation).reshape(shape)
        if axis == 1:
            low, mid, high = low[:, None, :], mid[:, None, :], high[:, None, :]
        else:
            low, mid, high = low[None, :, :], mid[None, :, :], high[None, :, :]
        return jnp.where(near_low, low, jnp.where(near_high, high, mid))

    mixed = (
        pick(rows_row_tables, col_places, 1) + pick(cols_col_tables, row_places, 0)
    ).astype(jnp.bfloat16)
    mixed_mirror = (
        pick(cols_row_tables, row_places, 0) + pick(rows_col_tables, col_places, 1)
    ).astype(jnp.bfloat16)
    return mixed, mixed_mirror, row_places, col_places


def local(features, row_weight, col_weight, conv_weight, conv_bias, dilations):
    both = jnp.concatenate([row_weight, col_weight], axis=1)
    proj = jnp.dot(features, both, preferred_element_type=jnp.float32).astype(jnp.bfloat16)
    every = gather_projections(proj)
    bins_total = every.shape[0]
    row_size = bins_total // lax.axis_size("row")
    col_size = bins_total // lax.axis_size("col")
    row_start = lax.axis_index("row") * row_size
    col_start = lax.axis_index("col") * col_size
    rows1 = row_size + 2 * MAXDIL
    cols1 = col_size + 2 * MAXDIL

    mixed0, mixed0_mirror, row_places, col_places = first_layer(
        every, conv_weight[0], conv_bias[0], dilations[0], row_start, rows1, col_start, cols1
    )
    map1 = (0.5 * (mixed0.astype(jnp.float32) + mixed0_mirror.astype(jnp.float32))).astype(
        jnp.bfloat16
    )

    mask1 = (
        inside(row_places, bins_total)[:, None, None] * inside(col_places, bins_total)[None, :, None]
    ).astype(jnp.bfloat16)
    taps1 = jnp.concatenate([conv_weight[1], mirrored_taps(conv_weight[1])], axis=1)
    conv1 = tap_groups(jax.nn.relu(map1) * mask1, taps1, dilations[1])
    channels = conv_weight.shape[2]
    core = (slice(MAXDIL, MAXDIL + row_size), slice(MAXDIL, MAXDIL + col_size), slice(None))
    base1 = map1[core].astype(jnp.float32) + conv_bias[1][None, None, :]
    mixed1 = (base1 + conv1[:, :, :channels]).astype(jnp.bfloat16)
    mixed1_mirror = (base1 + conv1[:, :, channels:]).astype(jnp.bfloat16)
    pair = (0.5 * (mixed1.astype(jnp.float32) + mixed1_mirror.astype(jnp.float32))).astype(
        jnp.bfloat16
    )
    turned = jnp.einsum(
        "ck,ijk->cij", jnp.eye(channels, dtype=pair.dtype), pair, preferred_element_type=jnp.float32
    )
    return turned.astype(jnp.bfloat16)


def solution(mesh):
    placed = (P(("row", "col"), None), P(), P(), P(), P(), P())
    return jax.shard_map(
        local, mesh=mesh, in_specs=placed, out_specs=P(None, "row", "col"), check_vma=False
    )
```

```python
import jax
import jax.numpy as jnp
from jax import lax
from jax.sharding import PartitionSpec as P

MAXDIL = 4
REACH = 2 * MAXDIL


def gather_projections(proj):
    axes = ("row", "col")
    count = lax.axis_size("row") * lax.axis_size("col")
    flat = proj.reshape(2, -1)
    copies = jnp.broadcast_to(flat[None], (count,) + flat.shape)
    return lax.all_to_all(copies, axes, 0, 0, tiled=True).reshape(-1, proj.shape[1])


def inside(places, bins_total):
    return ((places >= 0) & (places < bins_total)).astype(jnp.float32)


def tap_groups(padded, weights, dilation):
    out_channels = weights.shape[1]
    in_channels = weights.shape[2]
    row_count = padded.shape[0] - 2 * MAXDIL
    col_count = padded.shape[1] - 2 * MAXDIL
    zero_index = jnp.zeros((), jnp.int32)
    pieces = []
    for tap in range(9):
        row_index = MAXDIL + (tap // 3 - 1) * dilation
        col_index = MAXDIL + (tap % 3 - 1) * dilation
        piece = lax.dynamic_slice(
            padded, (row_index, col_index, zero_index), (row_count, col_count, in_channels)
        )
        pieces.append(piece.reshape(row_count * col_count, in_channels))
    stacked = jnp.concatenate(pieces, axis=1)
    flat_weight = jnp.transpose(weights, (0, 2, 1)).reshape(9 * in_channels, out_channels)
    summed = jnp.dot(stacked, flat_weight, preferred_element_type=jnp.float32)
    return summed.reshape(row_count, col_count, out_channels)


def mirrored_taps(weights):
    return weights.reshape(3, 3, *weights.shape[1:]).swapaxes(0, 1).reshape(weights.shape)


def first_layer(every, taps, shift_bias, dilation, row_start, rows, col_start, cols):
    bins_total = every.shape[0]
    half = every.shape[1] // 2
    lower = jnp.arange(every.shape[1]) < half
    active = jnp.pad(jax.nn.relu(every), ((REACH, REACH), (0, 0)))
    padded = jnp.pad(every, ((MAXDIL, MAXDIL), (0, 0)))

    grid = taps.reshape(3, 3, *taps.shape[1:])
    out_ch = taps.shape[1]
    by_shift_row = jnp.transpose(grid[..., :half], (0, 3, 1, 2)).reshape(3, half, 3 * out_ch)
    by_shift_col = jnp.transpose(grid[..., half:], (1, 3, 0, 2)).reshape(3, half, 3 * out_ch)
    lane_group = 2 * out_ch
    by_shift_row, by_shift_col = (
        jnp.pad(w.reshape(3, half, 3, out_ch), ((0, 0), (0, 0), (0, 0), (0, lane_group - out_ch))).reshape(
            3, half, 3 * lane_group
        )
        for w in (by_shift_row, by_shift_col)
    )
    nothing = jnp.zeros_like(by_shift_row)
    weight = jnp.concatenate(
        [
            jnp.concatenate([by_shift_row, nothing], axis=2),
            jnp.concatenate([nothing, by_shift_col], axis=2),
        ],
        axis=1,
    ).reshape(3 * 2 * half, 6 * lane_group)

    def shifted_rows(start, count):
        window = lax.dynamic_slice_in_dim(active, start, count + 2 * MAXDIL, 0)
        return jnp.concatenate(
            [
                lax.dynamic_slice_in_dim(window, MAXDIL + (step - 1) * dilation, count, 0)
                for step in range(3)
            ],
            axis=1,
        )

    def tables(start, count, parts):
        by_col = [parts[:, lane_group * k : lane_group * k + out_ch] for k in range(3)]
        by_row = [parts[:, lane_group * (3 + k) : lane_group * (3 + k) + out_ch] for k in range(3)]
        own = lax.dynamic_slice_in_dim(padded, start, count, 0)
        own_row = jnp.where(lower, own, 0.0) + shift_bias[None, :]
        own_col = jnp.where(lower, 0.0, own)
        row_tables = [
            own_row + by_col[1] + by_col[2],
            own_row + by_col[0] + by_col[1] + by_col[2],
            own_row + by_col[0] + by_col[1],
        ]
        col_tables = [
            own_col + by_row[1] + by_row[2],
            own_col + by_row[0] + by_row[1] + by_row[2],
            own_col + by_row[0] + by_row[1],
        ]
        return row_tables, col_tables

    row_places = row_start - MAXDIL + jnp.arange(rows)
    col_places = col_start - MAXDIL + jnp.arange(cols)
    both_parts = jnp.dot(
        jnp.concatenate([shifted_rows(row_start, rows), shifted_rows(col_start, cols)], axis=0),
        weight,
        preferred_element_type=jnp.float32,
    )
    rows_row_tables, rows_col_tables = tables(row_start, rows, both_parts[:rows])
    cols_row_tables, cols_col_tables = tables(col_start, cols, both_parts[rows:])

    def pick(tables_here, places, axis):
        low, mid, high = tables_here
        shape = [1, 1, 1]
        shape[axis] = -1
        near_low = (places < dilation).reshape(shape)
        near_high = (places >= bins_total - dilation).reshape(shape)
        if axis == 1:
            low, mid, high = low[:, None, :], mid[:, None, :], high[:, None, :]
        else:
            low, mid, high = low[None, :, :], mid[None, :, :], high[None, :, :]
        return jnp.where(near_low, low, jnp.where(near_high, high, mid))

    mixed = (
        pick(rows_row_tables, col_places, 1) + pick(cols_col_tables, row_places, 0)
    ).astype(jnp.bfloat16)
    mixed_mirror = (
        pick(cols_row_tables, row_places, 0) + pick(rows_col_tables, col_places, 1)
    ).astype(jnp.bfloat16)
    return mixed, mixed_mirror, row_places, col_places


def local(features, row_weight, col_weight, conv_weight, conv_bias, dilations):
    both = jnp.concatenate([row_weight, col_weight], axis=1)
    proj = jnp.dot(features, both, preferred_element_type=jnp.float32).astype(jnp.bfloat16)
    every = gather_projections(proj)
    bins_total = every.shape[0]
    row_size = bins_total // lax.axis_size("row")
    col_size = bins_total // lax.axis_size("col")
    row_start = lax.axis_index("row") * row_size
    col_start = lax.axis_index("col") * col_size
    rows1 = row_size + 2 * MAXDIL
    cols1 = col_size + 2 * MAXDIL

    mixed0, mixed0_mirror, row_places, col_places = first_layer(
        every, conv_weight[0], conv_bias[0], dilations[0], row_start, rows1, col_start, cols1
    )
    map1 = (0.5 * (mixed0.astype(jnp.float32) + mixed0_mirror.astype(jnp.float32))).astype(
        jnp.bfloat16
    )

    mask1 = (
        inside(row_places, bins_total)[:, None, None] * inside(col_places, bins_total)[None, :, None]
    ).astype(jnp.bfloat16)
    taps1 = jnp.concatenate([conv_weight[1], mirrored_taps(conv_weight[1])], axis=1)
    conv1 = tap_groups(jax.nn.relu(map1) * mask1, taps1, dilations[1])
    channels = conv_weight.shape[2]
    core = (slice(MAXDIL, MAXDIL + row_size), slice(MAXDIL, MAXDIL + col_size), slice(None))
    base1 = map1[core].astype(jnp.float32) + conv_bias[1][None, None, :]
    mixed1 = (base1 + conv1[:, :, :channels]).astype(jnp.bfloat16)
    mixed1_mirror = (base1 + conv1[:, :, channels:]).astype(jnp.bfloat16)
    pair = (0.5 * (mixed1.astype(jnp.float32) + mixed1_mirror.astype(jnp.float32))).astype(
        jnp.bfloat16
    )
    flat = pair.reshape(row_size * col_size, channels)
    turned = jnp.einsum(
        "ck,nk->cn", jnp.eye(channels, dtype=pair.dtype), flat, preferred_element_type=jnp.float32
    )
    return turned.astype(jnp.bfloat16).reshape(channels, row_size, col_size)


def solution(mesh):
    placed = (P(("row", "col"), None), P(), P(), P(), P(), P())
    return jax.shard_map(
        local, mesh=mesh, in_specs=placed, out_specs=P(None, "row", "col"), check_vma=False
    )
```
